256 devices in a mesh: leaf: 4 (over x), dof: 4 (over y), blk: 16 (over z, core).
Axes of the slice: x: 4, y: 4, z: 8, core: 2. Of those that a mesh axis runs over, the one named last changes fastest.
Arguments:
- modes: bfloat16 [4, 128, 128, 16, 128], P('leaf', 'blk', 'dof'), may hold values from -1.5 to 1.5
- stiffness: float32 [4, 128, 16, 128], P('leaf', 'dof'), may hold values from 0.25 to 2
- density: float32 [4, 128, 16, 128], P('leaf', 'dof'), may hold values from 0.5 to 4
- eigen_blocks: bfloat16 [4, 128, 128], P('leaf', None, 'blk'), may hold values from -0.5 to 0.5
- parent: int32 [4], replicated, may hold values from 0 to 1
Outputs:
- node_stiffness: float32 [2, 128, 128], P(None, 'blk')
- root_stiffness: float32 [128, 128], P('blk')
- leaf_vectors: bfloat16 [4, 128, 128, 16, 128], P('leaf', 'blk', 'dof')
The draws below stay inside these ranges and needn't reach their ends.
All inputs are finite; a program needn't handle non-finite values.
Results may differ from the reference program's by a relative error of at most 0.0035.
Values may be sent and summed in bfloat16 or wider, within the bound.
A program may use at most 64 MiB of HBM per device.

```python
import math
import jax
import jax.numpy as jnp
from jax import lax

MODES = 128
EIGS = 128
CY = 16
CZ = 128
LEAVES = 4
NODES = 2
NXL = 128


def draw_parent(key, part):
    base = jax.random.fold_in(key, 9173)
    first, second = jax.random.split(base)
    covered = jnp.arange(NODES, dtype=jnp.int32)
    others = jax.random.randint(first, (LEAVES - NODES,), 0, NODES, dtype=jnp.int32)
    labels = jnp.concatenate([covered, others])
    return jax.random.permutation(second, labels).astype(jnp.int32)


def draw_modes(key, part):
    base = jax.random.fold_in(key, 4411)
    keys = jax.random.split(base, 4)
    waves = jax.random.uniform(keys[0], (3, LEAVES, MODES), jnp.float32, 0.02, 0.25)
    phases = jax.random.uniform(keys[1], (3, LEAVES, MODES), jnp.float32, -math.pi, math.pi)
    x_cells = jnp.arange(NXL, dtype=jnp.float32)
    y_cells = jnp.arange(CY, dtype=jnp.float32)
    z_cells = jnp.arange(CZ, dtype=jnp.float32)
    along_x = jnp.cos(waves[0][:, :, None] * x_cells[None, None, :] + phases[0][:, :, None])
    along_y = jnp.cos(waves[1][:, :, None] * y_cells[None, None, :] + phases[1][:, :, None])
    along_z = jnp.cos(waves[2][:, :, None] * z_cells[None, None, :] + phases[2][:, :, None])
    smooth = along_x[:, :, :, None, None] * along_y[:, :, None, :, None] * along_z[:, :, None, None, :]
    shape = (LEAVES, MODES, NXL, CY, CZ)
    noise = 0.1 * jnp.clip(jax.random.normal(keys[3], shape, jnp.float32), -5.0, 5.0)
    field = smooth + noise
    return field.astype(jnp.bfloat16)


def level_of(stream_key, extent, pieces, least, high):
    def one(dim, parts):
        draws = jax.random.uniform(jax.random.fold_in(jax.random.fold_in(stream_key, 6), dim), (parts,), jnp.float32, least / len(pieces), high / len(pieces))
        return jnp.repeat(jnp.exp(draws), extent[dim] // parts).reshape((-1,) + (1,) * (len(extent) - dim - 1))

    level = one(*pieces[0])
    for cut in pieces[1:]:
        level = level * one(*cut)
    return level


def scatter_about(key, dims, spread, limit, cuts=(), kind=jnp.bfloat16):
    array = jax.random.normal(key, dims, jnp.float32) * spread
    if len(cuts) > 0:
        array = level_of(key, dims, cuts, -0.22, 0.18) * array
    return jnp.clip(array, min=-limit, max=limit).astype(kind)


def setup_inputs(seed: int = 0) -> dict:
    key_of = jax.random.split(jax.random.key(seed), 6)
    modes = draw_modes(jax.random.fold_in(key_of[5], 71), 0)
    stiffness = jnp.clip(0.25 + 1.75 * jax.random.uniform(key_of[1], (LEAVES, NXL, CY, CZ), jnp.float32) ** level_of(key_of[1], (LEAVES, NXL, CY, CZ), ((0, 4), (1, 4)), -0.2, 0.2), 0.25, 2.0)
    density = jnp.clip(jnp.exp(math.log(4.0) - 2.0794415 * jax.random.uniform(key_of[2], (LEAVES, NXL, CY, CZ), jnp.float32) ** level_of(key_of[2], (LEAVES, NXL, CY, CZ), ((0, 4), (1, 4)), -0.2, 0.2)), 0.5, 4.0)
    eigen_blocks = scatter_about(key_of[3], (LEAVES, MODES, EIGS), MODES ** -0.5, 0.5, ((0, 4), (2, 16)))
    parent = draw_parent(jax.random.fold_in(key_of[5], 71), 0)
    return {"modes": modes, "stiffness": stiffness, "density": density, "eigen_blocks": eigen_blocks, "parent": parent}


def neighbours(padded):
    inner = padded[:, 1:-1]
    sides = jnp.pad(inner, ((0, 0), (0, 0), (1, 1), (1, 1)))
    total = padded[:, 2:] + padded[:, :-2]
    total = total + sides[:, :, 2:, 1:-1] + sides[:, :, :-2, 1:-1]
    total = total + sides[:, :, 1:-1, 2:] + sides[:, :, 1:-1, :-2]
    return total

def leaf_terms(items):
    phi, coefs, masses, blocks = items
    field = phi.astype(jnp.float32)
    padded = jnp.pad(field, ((0, 0), (1, 1), (0, 0), (0, 0)))
    stiff = ((6.0 + coefs) * field - neighbours(padded)).astype(jnp.bfloat16)
    flat = phi.reshape(MODES, -1)
    reduced = lax.dot_general(stiff.reshape(MODES, -1), flat, (((1,), (1,)), ((), ())), preferred_element_type=jnp.float32)
    weighed = lax.optimization_barrier((masses * field).astype(jnp.bfloat16))
    diagonal = lax.optimization_barrier(jnp.sum(weighed.reshape(MODES, -1).astype(jnp.float32) * flat.astype(jnp.float32), axis=1))
    vectors = lax.dot_general(blocks, flat, (((0,), (0,)), ((), ())), preferred_element_type=jnp.float32)
    vectors = vectors.astype(jnp.bfloat16).reshape(EIGS, NXL, CY, CZ)
    return (reduced, diagonal, vectors)

def reference(modes, stiffness, density, eigen_blocks, parent):
    reduced, diagonal, vectors = lax.map(leaf_terms, (modes, stiffness, density, eigen_blocks))
    onehot = (parent[:, None] == jnp.arange(NODES, dtype=jnp.int32)[None, :]).astype(jnp.float32)
    node_stiffness = jnp.einsum('lp,lij->pij', onehot, reduced, precision=lax.Precision.HIGHEST)
    node_mass = jnp.einsum('lp,li->pi', onehot, diagonal, precision=lax.Precision.HIGHEST)
    scale = 1.0 / jnp.sqrt(node_mass)
    root_stiffness = lax.optimization_barrier(jnp.sum(scale[:, :, None] * node_stiffness * scale[:, None, :], axis=0))
    return (node_stiffness, root_stiffness, vectors)
```

```python
import jax
import jax.numpy as jnp
from jax import lax
from jax.experimental import pallas as pl
from jax.experimental.pallas import tpu as pltpu
from jax.sharding import PartitionSpec as P

MESH = pl.DeviceIdType.MESH
F32 = jnp.float32
BF16 = jnp.bfloat16


def ring_order(chips):
    half = chips // 2
    steps = [half] + [s for d in range(half - 1, 0, -1) for s in (d, chips - d)]
    return [(dz, dc) for dz in steps for dc in (0, 1)] + [(0, 1)]


def kernel(
    sizes,
    modes,
    stiffness,
    density,
    eigen,
    parent,
    node_out,
    root_out,
    vec_out,
    own,
    dens,
    coef,
    eig_in,
    eig_send,
    eig,
    land,
    wide,
    phi,
    lhs,
    tall,
    vecs,
    edge,
    kfull,
    ksend,
    kland,
    msend,
    mland,
    psend,
    pland,
    load_sem,
    in_send,
    in_recv,
    e_send,
    e_recv,
    out_send,
    out_recv,
    k_send,
    k_recv,
    m_send,
    m_recv,
    p_send,
    p_recv,
    h_send,
    h_recv,
):
    leaves, dofs, blks = sizes
    chips = blks // 2
    rows, layers, cy, cz = own.shape
    n_modes = rows * blks
    half = cy // 2
    x, y, b = lax.axis_index("leaf"), lax.axis_index("dof"), lax.axis_index("blk")
    z, c = b // 2, lax.rem(b, 2)

    def layer_of(zz, cc, h):
        return 4 * zz + (3 * cc if h == 0 else 1 + cc)

    def column_peer(dz, dc):
        zz = lax.rem(z + dz, chips)
        cc = lax.rem(c + dc, 2)
        return zz, cc, zz * 2 + cc

    peers = [column_peer(dz, dc) for dz, dc in ring_order(chips)]
    plane = [(i, j) for i in range(leaves) for j in range(dofs) if (i, j) != (0, 0)]
    plane = [(lax.rem(x + i, leaves), lax.rem(y + j, dofs)) for i, j in plane]

    step = 2 * c - 1
    pz_raw = z + step
    pz = lax.rem(pz_raw + chips, chips)
    wraps = jnp.where(c == 1, jnp.where(z == chips - 1, 1, 0), jnp.where(z == 0, 1, 0))
    py = lax.rem(y + step * wraps + dofs, dofs)
    pb = pz * 2 + (1 - c)
    at_end = jnp.where(c == 1, jnp.where(y == dofs - 1, 1, 0), jnp.where(y == 0, 1, 0)) * wraps
    edge_weight = jnp.where(at_end == 1, 0.0, -2.0).astype(F32)

    loads = [
        pltpu.make_async_copy(eigen.at[0], eig_in, load_sem.at[0]),
        pltpu.make_async_copy(modes.at[0], own, load_sem.at[1]),
        pltpu.make_async_copy(density.at[0], dens, load_sem.at[2]),
        pltpu.make_async_copy(stiffness.at[0, pl.ds(layer_of(z, c, 0), 1)], coef.at[pl.ds(0, 1)], load_sem.at[3]),
        pltpu.make_async_copy(stiffness.at[0, pl.ds(layer_of(z, c, 1), 1)], coef.at[pl.ds(1, 1)], load_sem.at[4]),
    ]
    for cp in loads:
        cp.start()

    barrier = pltpu.get_barrier_semaphore()
    for _, _, p in peers:
        pl.semaphore_signal(barrier, inc=1, device_id={"blk": p}, device_id_type=MESH)
    for i, j in plane:
        pl.semaphore_signal(barrier, inc=1, device_id={"leaf": i, "dof": j}, device_id_type=MESH)
    pl.semaphore_signal(barrier, inc=1, device_id={"dof": py, "blk": pb}, device_id_type=MESH)

    loads[0].wait()
    eig_t = eig_in[...].astype(F32).T
    eig_send[...] = eig_t
    my_rows = pl.ds(pl.multiple_of(b * rows, rows), rows)
    eig[my_rows, :] = eig_t

    pl.semaphore_wait(barrier, len(peers) + len(plane) + 1)

    e_copies = []
    in_copies = [[], []]
    for n, (zz, cc, p) in enumerate(peers):
        cp = pltpu.make_async_remote_copy(
            eig_send, eig.at[my_rows], e_send.at[n], e_recv.at[n], device_id={"blk": p}, device_id_type=MESH
        )
        cp.start()
        e_copies.append(cp)
    for h in range(2):
        for n, (zz, cc, p) in enumerate(peers):
            cp = pltpu.make_async_remote_copy(
                modes.at[0, :, layer_of(zz, cc, h)],
                land.at[h, my_rows],
                in_send.at[h, n],
                in_recv.at[h, n],
                device_id={"blk": p},
                device_id_type=MESH,
            )
            cp.start()
            in_copies[h].append(cp)
    local_in = [
        pltpu.make_async_copy(modes.at[0, :, layer_of(z, c, h)], land.at[h, my_rows], load_sem.at[5 + h])
        for h in range(2)
    ]
    for cp in local_in:
        cp.start()

    loads[1].wait()
    loads[2].wait()

    def mass_step(i, acc):
        f = own[:, i].astype(F32)
        w = (dens[i][None] * f).astype(BF16).astype(F32)
        return acc + w * f

    acc = lax.fori_loop(0, layers, mass_step, jnp.zeros((rows, cy, cz), F32))
    mass = jnp.sum(jnp.sum(acc, axis=1), axis=1, keepdims=True)
    lane = lax.broadcasted_iota(jnp.int32, (rows, n_modes), 1)
    sub = lax.broadcasted_iota(jnp.int32, (rows, n_modes), 0)
    mine = lane == sub + b * rows
    mass_row = jnp.sum(jnp.where(mine, mass, 0.0), axis=0, keepdims=True)
    msend[...] = mass_row
    m_copies = []
    for n, (_, _, p) in enumerate(peers):
        cp = pltpu.make_async_remote_copy(
            msend, mland.at[n], m_send.at[n], m_recv.at[n], device_id={"blk": p}, device_id_type=MESH
        )
        cp.start()
        m_copies.append(cp)
    loads[3].wait()
    loads[4].wait()

    last_lane = lax.broadcasted_iota(jnp.int32, (n_modes, cz), 1) == cz - 1

    def relayout(h):
        wide[...] = land[h].reshape(n_modes * cy, cz).astype(F32)
        for j in range(cy):
            phi[h, :, j * cz : (j + 1) * cz] = wide[pl.ds(j, n_modes, stride=cy), :].astype(BF16)

    def send_edge(h, device):
        cp = pltpu.make_async_remote_copy(
            phi.at[h, :, pl.ds(pl.multiple_of(c * half * cz, half * cz), half * cz)],
            edge.at[h],
            h_send.at[h],
            h_recv.at[h],
            device_id=device,
            device_id_type=MESH,
        )
        cp.start()
        return cp

    def expand(h):
        e = eig[...].astype(BF16)
        for j in range(0, cy, 2):
            v = jnp.dot(e, phi[h, :, j * cz : (j + 2) * cz], preferred_element_type=F32)
            tall[pl.ds(j, n_modes, stride=cy), :] = v[:, :cz]
            tall[pl.ds(j + 1, n_modes, stride=cy), :] = v[:, cz:]
        vecs[h] = tall[...].astype(BF16).reshape(n_modes, cy, cz)

    def send_vectors(h):
        cps = []
        for n, (_, _, p) in enumerate(peers):
            cp = pltpu.make_async_remote_copy(
                vecs.at[h, pl.ds(pl.multiple_of(p * rows, rows), rows)],
                vec_out.at[:, layer_of(z, c, h)],
                out_send.at[h, n],
                out_recv.at[h, n],
                device_id={"blk": p},
                device_id_type=MESH,
            )
            cp.start()
            cps.append(cp)
        cp = pltpu.make_async_copy(vecs.at[h, my_rows], vec_out.at[:, layer_of(z, c, h)], load_sem.at[7 + h])
        cp.start()
        return cps, cp

    def images(h, other):
        nxt = wide[pl.ds(0, n_modes, stride=cy), :]
        for j in range(cy):
            f = nxt
            s = coef[h, j : j + 1, :] + 6.0
            side = jnp.where(last_lane, 0.0, pltpu.roll(f, cz - 1, 1))
            if j + 1 < cy:
                nxt = wide[pl.ds(j + 1, n_modes, stride=cy), :]
                side = side + nxt
            if other is not None:
                side = side + phi[other, :, j * cz : (j + 1) * cz].astype(F32)
            lhs[:, j * cz : (j + 1) * cz] = (s * f - 2.0 * side).astype(BF16)
        return lax.dot_general(lhs[...], phi[h], (((1,), (1,)), ((), ())), preferred_element_type=F32)

    def edge_product(h):
        part = phi[h, :, pl.ds(pl.multiple_of((1 - c) * half * cz, half * cz), half * cz)]
        return lax.dot_general(edge[h], part, (((1,), (1,)), ((), ())), preferred_element_type=F32)

    for cp in in_copies[0]:
        cp.wait_recv()
    local_in[0].wait()
    relayout(0)
    edge0 = send_edge(0, {"dof": py, "blk": pb})
    for cp in e_copies:
        cp.wait_recv()
    expand(0)
    out0, local0 = send_vectors(0)
    kfull[...] = images(0, None)
    edge0.wait_recv()
    kfull[...] += edge_weight * edge_product(0)

    for cp in in_copies[1]:
        cp.wait_recv()
    local_in[1].wait()
    relayout(1)
    edge1 = send_edge(1, {"blk": z * 2 + (1 - c)})
    kfull[...] += images(1, 0)
    edge1.wait_recv()
    total = kfull[...] - 2.0 * edge_product(1)
    kfull[...] = 0.5 * (total + total.T)
    for i in range(blks):
        ksend[i] = kfull[i * rows : (i + 1) * rows, :].astype(BF16)
    k_copies = []
    for n, (_, _, p) in enumerate(peers):
        cp = pltpu.make_async_remote_copy(
            ksend.at[p], kland.at[n], k_send.at[n], k_recv.at[n], device_id={"blk": p}, device_id_type=MESH
        )
        cp.start()
        k_copies.append(cp)
    expand(1)
    out1, local1 = send_vectors(1)

    mass_total = mass_row
    for n, cp in enumerate(m_copies):
        cp.wait_recv()
        mass_total = mass_total + mland[n]
    k_total = ksend[b].astype(F32)
    for n, cp in enumerate(k_copies):
        cp.wait_recv()
        k_total = k_total + kland[n].astype(F32)
    psend[:rows] = k_total
    psend[rows:] = jnp.broadcast_to(mass_total, (rows, n_modes))
    p_copies = []
    slot = x * dofs + y
    for n, (i, j) in enumerate(plane):
        cp = pltpu.make_async_remote_copy(
            psend, pland.at[slot], p_send.at[n], p_recv.at[n], device_id={"leaf": i, "dof": j}, device_id_type=MESH
        )
        cp.start()
        p_copies.append(cp)
    pland[slot] = psend[...]
    for cp in p_copies:
        cp.wait_recv()
    per_leaf = []
    for i in range(leaves):
        t = pland[i * dofs]
        for j in range(1, dofs):
            t = t + pland[i * dofs + j]
        per_leaf.append(t)
    root = jnp.zeros((rows, n_modes), F32)
    for node in range(node_out.shape[0]):
        t = jnp.zeros((2 * rows, n_modes), F32)
        for i in range(leaves):
            t = t + jnp.where(parent[i] == node, 1.0, 0.0).astype(F32) * per_leaf[i]
        node_out[node] = t[:rows]
        scale = 1.0 / jnp.sqrt(t[rows:])
        scale_own = jnp.sum(jnp.where(mine, scale, 0.0), axis=1, keepdims=True)
        root = root + scale_own * t[:rows] * scale
    root_out[...] = root

    for cp in in_copies[0] + in_copies[1] + e_copies + m_copies + k_copies + p_copies + [edge0, edge1]:
        cp.wait_send()
    for cp in out0 + out1:
        cp.wait()
    local0.wait()
    local1.wait()


def solution(mesh):
    leaves, dofs, blks = (mesh.shape[a] for a in ("leaf", "dof", "blk"))

    def body(modes, stiffness, density, eigen_blocks, parent):
        _, rows, layers, cy, cz = modes.shape
        n_modes = rows * blks
        cells = cy * cz
        others = blks - 1
        planes = leaves * dofs - 1
        dma = pltpu.SemaphoreType.DMA
        any_spec = pl.BlockSpec(memory_space=pl.ANY)
        vmem_spec = pl.BlockSpec(memory_space=pltpu.VMEM)
        node, root, vectors = pl.pallas_call(
            lambda *refs: kernel((leaves, dofs, blks), *refs),
            out_shape=(
                jax.ShapeDtypeStruct((leaves // 2, rows, n_modes), F32),
                jax.ShapeDtypeStruct((rows, n_modes), F32),
                jax.ShapeDtypeStruct((rows, layers, cy, cz), BF16),
            ),
            in_specs=[any_spec] * 4 + [pl.BlockSpec(memory_space=pltpu.SMEM)],
            out_specs=(vmem_spec, vmem_spec, any_spec),
            scratch_shapes=[
                pltpu.VMEM((rows, layers, cy, cz), BF16),
                pltpu.VMEM((layers, cy, cz), F32),
                pltpu.VMEM((2, cy, cz), F32),
                pltpu.VMEM((n_modes, rows), BF16),
                pltpu.VMEM((rows, n_modes), F32),
                pltpu.VMEM((n_modes, n_modes), F32),
                pltpu.VMEM((2, n_modes, cy, cz), BF16),
                pltpu.VMEM((n_modes * cy, cz), F32),
                pltpu.VMEM((2, n_modes, cells), BF16),
                pltpu.VMEM((n_modes, cells), BF16),
                pltpu.VMEM((n_modes * cy, cz), F32),
                pltpu.VMEM((2, n_modes, cy, cz), BF16),
                pltpu.VMEM((2, n_modes, cells // 2), BF16),
                pltpu.VMEM((n_modes, n_modes), F32),
                pltpu.VMEM((blks, rows, n_modes), BF16),
                pltpu.VMEM((others, rows, n_modes), BF16),
                pltpu.VMEM((1, n_modes), F32),
                pltpu.VMEM((others, 1, n_modes), F32),
                pltpu.VMEM((2 * rows, n_modes), F32),
                pltpu.VMEM((leaves * dofs, 2 * rows, n_modes), F32),
                dma((9,)),
                dma((2, others)),
                dma((2, others)),
                dma((others,)),
                dma((others,)),
                dma((2, others)),
                dma((2, others)),
                dma((others,)),
                dma((others,)),
                dma((others,)),
                dma((others,)),
                dma((planes,)),
                dma((planes,)),
                dma((2,)),
                dma((2,)),
            ],
            compiler_params=pltpu.CompilerParams(collective_id=0, has_side_effects=True),
            name="tree",
        )(modes, stiffness, density, eigen_blocks, parent)
        return node, root, vectors[None]

    in_specs = (
        P("leaf", "blk", "dof", None, None),
        P("leaf", "dof", None, None),
        P("leaf", "dof", None, None),
        P("leaf", None, "blk"),
        P(),
    )
    out_specs = (P(None, "blk", None), P("blk", None), P("leaf", "blk", "dof", None, None))
    return jax.shard_map(body, mesh=mesh, in_specs=in_specs, out_specs=out_specs, check_vma=False)
```

```python
import jax
import jax.numpy as jnp
from jax import lax
from jax.experimental import pallas as pl
from jax.experimental.pallas import tpu as pltpu
from jax.sharding import PartitionSpec as P

MESH = pl.DeviceIdType.MESH
F32 = jnp.float32
BF16 = jnp.bfloat16
FIRST_PART = 8


def ring_peers(chips):
    found = {}
    for dz in range(chips):
        for dc in range(2):
            if dz or dc:
                found.setdefault(min(dz, chips - dz) + dc, []).append((dz, dc))
    return [found[d] for d in sorted(found)]


def drain(ref, sem):
    pltpu.make_async_copy(ref, ref, sem).wait()


def kernel(
    sizes,
    first_part,
    modes,
    stiffness,
    density,
    eigen,
    parent_in,
    node_out,
    root_out,
    vec_out,
    parent,
    node,
    root_sum,
    own,
    dens,
    coef,
    eig_in,
    eig,
    land,
    wide,
    phi,
    lhs,
    tall,
    vecs,
    edge,
    kfull,
    ksend,
    kland,
    msend,
    mland,
    psend,
    pland,
    load_sem,
    in_recv,
    out_recv,
    h_recv,
    small_recv,
    send_sem,
    near_sem,
    plane_sem,
):
    leaves, dofs, blks = sizes
    chips = blks // 2
    rows, layers, cy, cz = own.shape
    n_modes = rows * blks
    half = cy // 2
    x, y, b = lax.axis_index("leaf"), lax.axis_index("dof"), lax.axis_index("blk")
    z, c = b // 2, lax.rem(b, 2)
    e_recv, k_recv, m_recv, p_recv = (small_recv.at[i] for i in range(4))
    in_send, e_send, out_send, k_send, m_send, p_send, h0_send, h1_send = (send_sem.at[i] for i in range(8))
    my_rows = pl.ds(pl.multiple_of(b * rows, rows), rows)

    def layer_of(zz, cc, h):
        return 4 * zz + (3 * cc if h == 0 else 1 + cc)

    def column_peer(dz, dc):
        zz = lax.rem(z + dz, chips)
        cc = lax.rem(c + dc, 2)
        return zz, cc, zz * 2 + cc

    rings = [[column_peer(dz, dc) for dz, dc in ring] for ring in ring_peers(chips)]
    peers = [p for ring in rings for p in ring]
    plane = [(i, j) for i in range(leaves) for j in range(dofs) if (i, j) != (0, 0)]
    plane = [(lax.rem(x + i, leaves), lax.rem(y + j, dofs)) for i, j in plane]

    step = 2 * c - 1
    pz = lax.rem(z + step + chips, chips)
    wraps = jnp.where(c == 1, jnp.where(z == chips - 1, 1, 0), jnp.where(z == 0, 1, 0))
    py = lax.rem(y + step * wraps + dofs, dofs)
    pb = pz * 2 + (1 - c)
    at_end = jnp.where(c == 1, jnp.where(y == dofs - 1, 1, 0), jnp.where(y == 0, 1, 0)) * wraps
    edge_weight = jnp.where(at_end == 1, 0.0, -2.0).astype(F32)

    near = [{"blk": p} for _, _, p in rings[0]]
    beside = [
        {"leaf": lax.rem(x + 1, leaves)},
        {"leaf": lax.rem(x + leaves - 1, leaves)},
        {"dof": lax.rem(y + 1, dofs)},
        {"dof": lax.rem(y + dofs - 1, dofs)},
    ]

    def tell(sem, devices):
        for device in devices:
            pl.semaphore_signal(sem, inc=1, device_id=device, device_id_type=MESH)

    barrier = pltpu.get_barrier_semaphore()
    tell(barrier, near + beside)
    loads = [
        pltpu.make_async_copy(eigen.at[0], eig_in, load_sem.at[0]),
        pltpu.make_async_copy(modes.at[0], own, load_sem.at[1]),
        pltpu.make_async_copy(density.at[0], dens, load_sem.at[2]),
        pltpu.make_async_copy(parent_in, parent, load_sem.at[3]),
        pltpu.make_async_copy(stiffness.at[0, pl.ds(layer_of(z, c, 0), 1)], coef.at[pl.ds(0, 1)], load_sem.at[4]),
        pltpu.make_async_copy(stiffness.at[0, pl.ds(layer_of(z, c, 1), 1)], coef.at[pl.ds(1, 1)], load_sem.at[4]),
    ]
    for cp in loads:
        cp.start()

    def remote(src, dst, send, recv, device):
        pltpu.make_async_remote_copy(src, dst, send, recv, device_id=device, device_id_type=MESH).start()

    def send_modes(h, peer):
        zz, cc, p = peer
        remote(modes.at[0, :, layer_of(zz, cc, h)], land.at[h, my_rows], in_send, in_recv.at[h], {"blk": p})

    pl.semaphore_wait(barrier, len(near) + len(beside))
    for r, ring in enumerate(rings):
        if r:
            pl.semaphore_wait(near_sem.at[r - 1], len(near))
        if r < len(rings) - 1:
            tell(near_sem.at[r], near)
        for peer in ring:
            send_modes(0, peer)
    loads[0].wait()
    for _, _, p in peers:
        remote(eig_in, eig.at[b], e_send, e_recv, {"blk": p})
    eig[b] = eig_in[...]
    for h in range(2):
        pltpu.make_async_copy(modes.at[0, :, layer_of(z, c, h)], land.at[h, my_rows], in_recv.at[h]).start()
    for peer in peers:
        send_modes(1, peer)

    loads[1].wait()
    loads[2].wait()

    def mass_step(i, acc):
        f = own[:, i].astype(F32)
        w = (dens[i][None] * f).astype(BF16).astype(F32)
        return acc + w * f

    acc = lax.fori_loop(0, layers, mass_step, jnp.zeros((rows, cy, cz), F32))
    mass = jnp.sum(jnp.sum(acc, axis=1), axis=1, keepdims=True)
    lane = lax.broadcasted_iota(jnp.int32, (rows, n_modes), 1)
    sub = lax.broadcasted_iota(jnp.int32, (rows, n_modes), 0)
    mine = lane == sub + b * rows
    mass_row = jnp.sum(jnp.where(mine, mass, 0.0), axis=0, keepdims=True)
    msend[...] = mass_row
    for n, (_, _, p) in enumerate(peers):
        remote(msend, mland.at[n], m_send, m_recv, {"blk": p})
    loads[3].wait()
    drain(coef, load_sem.at[4])
    rounds = leaves // 2 + dofs // 2 - 1
    for r in range(rounds):
        tell(plane_sem.at[r], beside)
        pl.semaphore_wait(plane_sem.at[r], len(beside))

    last_lane = lax.broadcasted_iota(jnp.int32, (n_modes, cz), 1) == cz - 1

    def relayout(h):
        wide[...] = land[h].reshape(n_modes * cy, cz).astype(F32)
        for j in range(cy):
            phi[h, :, j * cz : (j + 1) * cz] = wide[pl.ds(j, n_modes, stride=cy), :].astype(BF16)

    def send_edge(h, send, device):
        part = phi.at[h, :, pl.ds(pl.multiple_of(c * half * cz, half * cz), half * cz)]
        remote(part, edge.at[h], send, h_recv.at[h], device)

    def expand(h):
        e = eig[...].astype(F32).reshape(n_modes, n_modes).astype(BF16)
        for j in range(0, cy, 2):
            v = jnp.dot(e, phi[h, :, j * cz : (j + 2) * cz], preferred_element_type=F32)
            tall[pl.ds(j, n_modes, stride=cy), :] = v[:, :cz]
            tall[pl.ds(j + 1, n_modes, stride=cy), :] = v[:, cz:]
        vecs[h] = tall[...].astype(BF16).reshape(n_modes, cy, cz)
        pltpu.make_async_copy(vecs.at[h, my_rows], vec_out.at[:, layer_of(z, c, h)], out_recv).start()

    def send_vectors(h, some):
        for _, _, p in some:
            block = vecs.at[h, pl.ds(pl.multiple_of(p * rows, rows), rows)]
            remote(block, vec_out.at[:, layer_of(z, c, h)], out_send, out_recv, {"blk": p})

    def images(h, other):
        nxt = wide[pl.ds(0, n_modes, stride=cy), :]
        for j in range(cy):
            f = nxt
            s = coef[h, j : j + 1, :] + 6.0
            side = jnp.where(last_lane, 0.0, pltpu.roll(f, cz - 1, 1))
            if j + 1 < cy:
                nxt = wide[pl.ds(j + 1, n_modes, stride=cy), :]
                side = side + nxt
            if other is not None:
                side = side + phi[other, :, j * cz : (j + 1) * cz].astype(F32)
            lhs[:, j * cz : (j + 1) * cz] = (s * f - 2.0 * side).astype(BF16)
        return lax.dot_general(lhs[...], phi[h], (((1,), (1,)), ((), ())), preferred_element_type=F32)

    def edge_product(h):
        part = phi[h, :, pl.ds(pl.multiple_of((1 - c) * half * cz, half * cz), half * cz)]
        return lax.dot_general(edge[h], part, (((1,), (1,)), ((), ())), preferred_element_type=F32)

    out_order = peers[::-1]
    drain(land.at[0], in_recv.at[0])
    relayout(0)
    send_edge(0, h0_send, {"dof": py, "blk": pb})
    drain(eig.at[pl.ds(0, blks - 1)], e_recv)
    expand(0)
    send_vectors(0, out_order[:first_part])
    kfull[...] = images(0, None)

    drain(land.at[1], in_recv.at[1])
    relayout(1)
    send_edge(1, h1_send, {"blk": z * 2 + (1 - c)})
    kfull[...] += images(1, 0)
    drain(edge.at[0], h_recv.at[0])
    kfull[...] += edge_weight * edge_product(0)
    drain(edge.at[1], h_recv.at[1])
    total = kfull[...] - 2.0 * edge_product(1)
    kfull[...] = 0.5 * (total + total.T)
    for i in range(blks):
        ksend[i] = kfull[i * rows : (i + 1) * rows, :].astype(BF16)
    for n, (_, _, p) in enumerate(peers):
        remote(ksend.at[p], kland.at[n], k_send, k_recv, {"blk": p})
    send_vectors(0, out_order[first_part:])
    expand(1)
    send_vectors(1, out_order)

    drain(mland, m_recv)
    mass_total = mass_row
    for n in range(blks - 1):
        mass_total = mass_total + mland[n]
    drain(kland, k_recv)
    k_total = ksend[b].astype(F32)
    for n in range(blks - 1):
        k_total = k_total + kland[n].astype(F32)
    psend[:rows] = k_total
    psend[rows:] = jnp.broadcast_to(mass_total, (rows, n_modes))
    slot = x * dofs + y
    for i, j in plane:
        remote(psend, pland.at[slot], p_send, p_recv, {"leaf": i, "dof": j})
    pland[slot] = psend[...]
    drain(pland.at[pl.ds(0, leaves * dofs - 1)], p_recv)

    per_leaf = []
    for i in range(leaves):
        t = pland[i * dofs]
        for j in range(1, dofs):
            t = t + pland[i * dofs + j]
        per_leaf.append(t)
    root = jnp.zeros((rows, n_modes), F32)
    for i_node in range(node.shape[0]):
        t = jnp.zeros((2 * rows, n_modes), F32)
        for i in range(leaves):
            t = t + jnp.where(parent[i] == i_node, 1.0, 0.0).astype(F32) * per_leaf[i]
        node[i_node] = t[:rows]
        scale = 1.0 / jnp.sqrt(t[rows:])
        scale_own = jnp.sum(jnp.where(mine, scale, 0.0), axis=1, keepdims=True)
        root = root + scale_own * t[:rows] * scale
    root_sum[...] = root
    results = [
        pltpu.make_async_copy(node, node_out, load_sem.at[5]),
        pltpu.make_async_copy(root_sum, root_out, load_sem.at[6]),
    ]
    for cp in results:
        cp.start()

    drain(modes.at[0, :, pl.ds(0, 2 * blks - 2)], in_send)
    drain(eig.at[pl.ds(0, blks - 1)], e_send)
    drain(kland, k_send)
    drain(mland, m_send)
    drain(pland.at[pl.ds(0, leaves * dofs - 1)], p_send)
    drain(edge.at[0], h0_send)
    drain(edge.at[1], h1_send)
    for cp in results:
        cp.wait()
    drain(modes.at[0, :, pl.ds(0, 2 * blks - 2)], out_send)
    drain(vec_out, out_recv)


def finish(*refs):
    count = len(refs) // 2
    sem = refs[-1]
    cps = [pltpu.make_async_copy(refs[i], refs[count + i], sem.at[i]) for i in range(count)]
    for cp in cps:
        cp.start()
    for cp in cps:
        cp.wait()


def solution(mesh):
    leaves, dofs, blks = (mesh.shape[a] for a in ("leaf", "dof", "blk"))

    def body(modes, stiffness, density, eigen_blocks, parent):
        _, rows, layers, cy, cz = modes.shape
        n_modes = rows * blks
        cells = cy * cz
        others = blks - 1
        dma = pltpu.SemaphoreType.DMA
        any_spec = pl.BlockSpec(memory_space=pl.ANY)
        vmem_spec = pl.BlockSpec(memory_space=pltpu.VMEM)
        shapes = (
            jax.ShapeDtypeStruct((leaves // 2, rows, n_modes), F32),
            jax.ShapeDtypeStruct((rows, n_modes), F32),
            jax.ShapeDtypeStruct((rows, layers, cy, cz), BF16),
        )
        results = pl.pallas_call(
            lambda *refs: kernel((leaves, dofs, blks), FIRST_PART, *refs),
            out_shape=tuple(pltpu.VMEM(s.shape, s.dtype) for s in shapes),
            in_specs=[any_spec] * 5,
            out_specs=(any_spec,) * 3,
            scratch_shapes=[
                pltpu.SMEM((leaves,), jnp.int32),
                pltpu.VMEM((leaves // 2, rows, n_modes), F32),
                pltpu.VMEM((rows, n_modes), F32),
                pltpu.VMEM((rows, layers, cy, cz), BF16),
                pltpu.VMEM((layers, cy, cz), F32),
                pltpu.VMEM((2, cy, cz), F32),
                pltpu.VMEM((rows, n_modes), BF16),
                pltpu.VMEM((blks, rows, n_modes), BF16),
                pltpu.VMEM((2, n_modes, cy, cz), BF16),
                pltpu.VMEM((n_modes * cy, cz), F32),
                pltpu.VMEM((2, n_modes, cells), BF16),
                pltpu.VMEM((n_modes, cells), BF16),
                pltpu.VMEM((n_modes * cy, cz), F32),
                pltpu.VMEM((2, n_modes, cy, cz), BF16),
                pltpu.VMEM((2, n_modes, cells // 2), BF16),
                pltpu.VMEM((n_modes, n_modes), F32),
                pltpu.VMEM((blks, rows, n_modes), BF16),
                pltpu.VMEM((others, rows, n_modes), BF16),
                pltpu.VMEM((1, n_modes), F32),
                pltpu.VMEM((others, 1, n_modes), F32),
                pltpu.VMEM((2 * rows, n_modes), F32),
                pltpu.VMEM((leaves * dofs, 2 * rows, n_modes), F32),
                dma((7,)),
                dma((2,)),
                dma(()),
                dma((2,)),
                dma((4,)),
                dma((8,)),
                pltpu.SemaphoreType.REGULAR((blks // 4,)),
                pltpu.SemaphoreType.REGULAR((leaves // 2 + dofs // 2 - 1,)),
            ],
            compiler_params=pltpu.CompilerParams(
                collective_id=0, has_side_effects=True
            ),
            name="tree",
        )(modes, stiffness, density, jnp.swapaxes(eigen_blocks, 1, 2), parent)
        node, root, vectors = pl.pallas_call(
            finish,
            out_shape=shapes,
            in_specs=[vmem_spec] * 3,
            out_specs=(any_spec,) * 3,
            scratch_shapes=[dma((3,))],
            compiler_params=pltpu.CompilerParams(vmem_limit_bytes=4 << 20),
            name="finish",
        )(*results)
        return node, root, vectors[None]

    in_specs = (
        P("leaf", "blk", "dof", None, None),
        P("leaf", "dof", None, None),
        P("leaf", "dof", None, None),
        P("leaf", None, "blk"),
        P(),
    )
    out_specs = (P(None, "blk", None), P("blk", None), P("leaf", "blk", "dof", None, None))
    return jax.shard_map(body, mesh=mesh, in_specs=in_specs, out_specs=out_specs, check_vma=False)
```

```python
import jax
import jax.numpy as jnp
from jax import lax
from jax.experimental import pallas as pl
from jax.experimental.pallas import tpu as pltpu
from jax.sharding import PartitionSpec as P

MESH = pl.DeviceIdType.MESH
F32 = jnp.float32
BF16 = jnp.bfloat16
FIRST_PART = 9
IN_PART = 12


def ring_peers(chips):
    found = {}
    for dz in range(chips):
        for dc in range(2):
            if dz or dc:
                found.setdefault(min(dz, chips - dz) + dc, []).append((dz, dc))
    return [found[d] for d in sorted(found)]


def drain(ref, sem):
    pltpu.make_async_copy(ref, ref, sem).wait()


def kernel(
    sizes,
    first_part,
    modes,
    stiffness,
    density,
    eigen,
    parent_in,
    node_out,
    root_out,
    vec_out,
    parent,
    node,
    root_sum,
    own,
    dens,
    coef,
    eig,
    land,
    wide,
    phi,
    lhs,
    tall,
    vecs,
    edge,
    kfull,
    ksend,
    kland,
    msend,
    mland,
    psend,
    pland,
    load_sem,
    in_recv,
    out_recv,
    h_recv,
    small_recv,
    send_sem,
    near_sem,
    plane_sem,
):
    leaves, dofs, blks = sizes
    chips = blks // 2
    rows, layers, cy, cz = own.shape
    n_modes = rows * blks
    half = cy // 2
    x, y, b = lax.axis_index("leaf"), lax.axis_index("dof"), lax.axis_index("blk")
    z, c = b // 2, lax.rem(b, 2)
    e_recv, k_recv, m_recv, p_recv, f_recv = (small_recv.at[i] for i in range(5))
    in_send, e_send, out_send, k_send, m_send, p_send, h0_send, h1_send, f_send = (send_sem.at[i] for i in range(9))
    my_rows = pl.ds(pl.multiple_of(b * rows, rows), rows)

    def layer_of(zz, cc, h):
        return 4 * zz + (3 * cc if h == 0 else 1 + cc)

    def column_peer(dz, dc):
        zz = lax.rem(z + dz, chips)
        cc = 1 - c if dc else c
        return zz, cc, zz * 2 + cc

    rings = [[column_peer(dz, dc) for dz, dc in ring] for ring in ring_peers(chips)]
    peers = [p for ring in rings for p in ring]
    plane = [(i, j) for i in range(leaves) for j in range(dofs) if (i, j) != (0, 0)]
    plane = [(lax.rem(x + i, leaves), lax.rem(y + j, dofs)) for i, j in plane]

    step = 2 * c - 1
    pz = lax.rem(z + step + chips, chips)
    wraps = jnp.where(c == 1, jnp.where(z == chips - 1, 1, 0), jnp.where(z == 0, 1, 0))
    py = lax.rem(y + step * wraps + dofs, dofs)
    pb = pz * 2 + (1 - c)
    at_end = jnp.where(c == 1, jnp.where(y == dofs - 1, 1, 0), jnp.where(y == 0, 1, 0)) * wraps

    near = [{"blk": p} for _, _, p in rings[0]]
    beside = [
        {"leaf": lax.rem(x + 1, leaves)},
        {"leaf": lax.rem(x + leaves - 1, leaves)},
        {"dof": lax.rem(y + 1, dofs)},
        {"dof": lax.rem(y + dofs - 1, dofs)},
    ]

    def tell(sem, devices):
        for device in devices:
            pl.semaphore_signal(sem, inc=1, device_id=device, device_id_type=MESH)

    def ahead(sem, up):
        for axis, i, n in (("leaf", x, leaves), ("dof", y, dofs)):
            step, first, last = (1, 0, n - 1) if up else (-1, n - 1, 0)

            @pl.when(i != last)
            def _():
                tell(sem, [{axis: i + step}])

            @pl.when(i == first)
            def _():
                tell(sem, [{axis: last}])

    def one(condition):
        return jnp.where(condition, 1, 0)

    heard_up = one(x > 0) + one(x == leaves - 1) + one(y > 0) + one(y == dofs - 1)
    heard_down = 2 * 2 - heard_up

    barrier = pltpu.get_barrier_semaphore()
    tell(barrier, near)
    ahead(barrier, True)
    loads = [
        pltpu.make_async_copy(modes.at[0], own, load_sem.at[0]),
        pltpu.make_async_copy(density.at[0], dens, load_sem.at[1]),
        pltpu.make_async_copy(parent_in, parent, load_sem.at[2]),
        pltpu.make_async_copy(stiffness.at[0, pl.ds(layer_of(z, c, 0), 1)], coef.at[pl.ds(0, 1)], load_sem.at[3]),
        pltpu.make_async_copy(stiffness.at[0, pl.ds(layer_of(z, c, 1), 1)], coef.at[pl.ds(1, 1)], load_sem.at[3]),
    ]
    for cp in loads:
        cp.start()

    def remote(src, dst, send, recv, device):
        pltpu.make_async_remote_copy(src, dst, send, recv, device_id=device, device_id_type=MESH).start()

    def send_modes(h, peer):
        zz, cc, p = peer
        remote(modes.at[0, :, layer_of(zz, cc, h)], land.at[h, my_rows], in_send, in_recv.at[h], {"blk": p})

    pl.semaphore_wait(barrier, heard_up + len(near))
    early, late = [], []
    for r, ring in enumerate(rings):
        if r:
            pl.semaphore_wait(near_sem.at[r - 1], len(near))
        if r < len(rings) - 1:
            tell(near_sem.at[r], near)
        if r == 0:
            ahead(plane_sem.at[0], False)
        for peer in ring:
            send_modes(0, peer)
            if r == 0:
                send_modes(1, peer)
                early.append(peer)
            else:
                late.insert(0, peer)
        for zz, cc, p in ring:
            if cc is c:
                remote(eigen.at[0], eig.at[c, z], e_send, e_recv, {"blk": p})
    for h in range(2):
        pltpu.make_async_copy(modes.at[0, :, layer_of(z, c, h)], land.at[h, my_rows], in_recv.at[h]).start()
    pltpu.make_async_copy(eigen.at[0], eig.at[c, z], e_recv).start()
    for peer in late[:IN_PART]:
        send_modes(1, peer)

    loads[0].wait()
    loads[1].wait()

    def mass_step(i, acc):
        f = own[:, i].astype(F32)
        w = (dens[i][None] * f).astype(BF16).astype(F32)
        return acc + w * f

    acc = lax.fori_loop(0, layers, mass_step, jnp.zeros((rows, cy, cz), F32))
    mass = jnp.sum(jnp.sum(acc, axis=1), axis=1, keepdims=True)
    lane = lax.broadcasted_iota(jnp.int32, (rows, n_modes), 1)
    sub = lax.broadcasted_iota(jnp.int32, (rows, n_modes), 0)
    mine = lane == sub + b * rows
    mass_row = jnp.sum(jnp.where(mine, mass, 0.0), axis=0, keepdims=True)
    msend[...] = mass_row
    for n, (_, _, p) in enumerate(peers):
        remote(msend, mland.at[n], m_send, m_recv, {"blk": p})
    loads[2].wait()
    drain(coef, load_sem.at[3])
    def plane_round(r):
        tell(plane_sem.at[r], beside)
        pl.semaphore_wait(plane_sem.at[r], len(beside))


    @pl.when(heard_down > 0)
    def _():
        pl.semaphore_wait(plane_sem.at[0], heard_down)

    plane_round(1)

    last_lane = lax.broadcasted_iota(jnp.int32, (n_modes, cz), 1) == cz - 1

    def relayout(h):
        wide[...] = land[h].reshape(n_modes * cy, cz).astype(F32)
        for j in range(cy):
            phi[h, :, j * cz : (j + 1) * cz] = wide[pl.ds(j, n_modes, stride=cy), :].astype(BF16)

    def send_edge(h, send, device):
        part = phi.at[h, :, pl.ds(pl.multiple_of(c * half * cz, half * cz), half * cz)]
        remote(part, edge.at[h], send, h_recv.at[h], device)

    def block_of(zz, cc):
        return pl.ds(pl.multiple_of((cc * chips + zz) * rows, rows), rows)

    def expand(h):
        e = eig[...].astype(F32).reshape(n_modes, n_modes).astype(BF16)
        for j in range(0, cy, 2):
            v = jnp.dot(e, phi[h, :, j * cz : (j + 2) * cz], preferred_element_type=F32)
            tall[pl.ds(j, n_modes, stride=cy), :] = v[:, :cz]
            tall[pl.ds(j + 1, n_modes, stride=cy), :] = v[:, cz:]
        vecs[h] = tall[...].astype(BF16).reshape(n_modes, cy, cz)
        pltpu.make_async_copy(vecs.at[h, block_of(z, c)], vec_out.at[:, layer_of(z, c, h)], out_recv).start()

    def send_vectors(h, some):
        for zz, cc, p in some:
            remote(vecs.at[h, block_of(zz, cc)], vec_out.at[:, layer_of(z, c, h)], out_send, out_recv, {"blk": p})

    def images(h, other):
        nxt = wide[pl.ds(0, n_modes, stride=cy), :]
        for j in range(cy):
            f = nxt
            s = coef[h, j : j + 1, :] + 6.0
            side = jnp.where(last_lane, 0.0, pltpu.roll(f, cz - 1, 1))
            if j + 1 < cy:
                nxt = wide[pl.ds(j + 1, n_modes, stride=cy), :]
                side = side + nxt
            if other is not None:
                side = side + phi[other, :, j * cz : (j + 1) * cz].astype(F32)
            lhs[:, j * cz : (j + 1) * cz] = (s * f - 2.0 * side).astype(BF16)
        return lax.dot_general(lhs[...], phi[h], (((1,), (1,)), ((), ())), preferred_element_type=F32)

    def edge_product(h):
        part = phi[h, :, pl.ds(pl.multiple_of((1 - c) * half * cz, half * cz), half * cz)]
        return lax.dot_general(edge[h], part, (((1,), (1,)), ((), ())), preferred_element_type=F32)

    out_order = peers[::-1]
    drain(land.at[0], in_recv.at[0])
    relayout(0)

    @pl.when(at_end == 0)
    def _():
        send_edge(0, h0_send, {"dof": py, "blk": pb})

    for peer in late[IN_PART:]:
        send_modes(1, peer)
    drain(eig.at[0], e_recv)
    remote(eig.at[c], eig.at[c], f_send, f_recv, {"blk": z * 2 + (1 - c)})
    kfull[...] = images(0, None)
    drain(eig.at[0], f_recv)
    expand(0)
    send_vectors(0, out_order[:first_part])
    for r in range(2, leaves // 2 + dofs // 2):
        plane_round(r)

    drain(land.at[1], in_recv.at[1])
    relayout(1)
    send_edge(1, h1_send, {"blk": z * 2 + (1 - c)})
    kfull[...] += images(1, 0)

    @pl.when(at_end == 0)
    def _():
        drain(edge.at[0], h_recv.at[0])
        kfull[...] -= 2.0 * edge_product(0)

    drain(edge.at[1], h_recv.at[1])
    total = kfull[...] - 2.0 * edge_product(1)
    kfull[...] = 0.5 * (total + total.T)
    for i in range(blks):
        ksend[i] = kfull[i * rows : (i + 1) * rows, :].astype(BF16)
    for n, (_, _, p) in enumerate(peers):
        remote(ksend.at[p], kland.at[n], k_send, k_recv, {"blk": p})
    send_vectors(0, out_order[first_part:])
    expand(1)
    send_vectors(1, out_order)

    drain(mland, m_recv)
    mass_total = mass_row
    for n in range(blks - 1):
        mass_total = mass_total + mland[n]
    drain(kland, k_recv)
    k_total = ksend[b].astype(F32)
    for n in range(blks - 1):
        k_total = k_total + kland[n].astype(F32)
    psend[:rows] = k_total
    psend[rows:] = jnp.broadcast_to(mass_total, (rows, n_modes))
    slot = x * dofs + y
    for i, j in plane:
        remote(psend, pland.at[slot], p_send, p_recv, {"leaf": i, "dof": j})
    pland[slot] = psend[...]
    drain(pland.at[pl.ds(0, leaves * dofs - 1)], p_recv)

    per_leaf = []
    for i in range(leaves):
        t = pland[i * dofs]
        for j in range(1, dofs):
            t = t + pland[i * dofs + j]
        per_leaf.append(t)
    root = jnp.zeros((rows, n_modes), F32)
    for i_node in range(node.shape[0]):
        t = jnp.zeros((2 * rows, n_modes), F32)
        for i in range(leaves):
            t = t + jnp.where(parent[i] == i_node, 1.0, 0.0).astype(F32) * per_leaf[i]
        node[i_node] = t[:rows]
        scale = 1.0 / jnp.sqrt(t[rows:])
        scale_own = jnp.sum(jnp.where(mine, scale, 0.0), axis=1, keepdims=True)
        root = root + scale_own * t[:rows] * scale
    root_sum[...] = root
    results = [
        pltpu.make_async_copy(node, node_out, load_sem.at[4]),
        pltpu.make_async_copy(root_sum, root_out, load_sem.at[5]),
    ]
    for cp in results:
        cp.start()

    drain(modes.at[0, :, pl.ds(0, 2 * blks - 2)], in_send)
    drain(eig.at[0, pl.ds(0, chips - 1)], e_send)
    drain(eig.at[0], f_send)
    drain(kland, k_send)
    drain(mland, m_send)
    drain(pland.at[pl.ds(0, leaves * dofs - 1)], p_send)

    @pl.when(at_end == 0)
    def _():
        drain(edge.at[0], h0_send)

    drain(edge.at[1], h1_send)
    for cp in results:
        cp.wait()
    drain(modes.at[0, :, pl.ds(0, 2 * blks - 2)], out_send)
    drain(vec_out, out_recv)


def finish(*refs):
    count = len(refs) // 2
    sem = refs[-1]
    cps = [pltpu.make_async_copy(refs[i], refs[count + i], sem.at[i]) for i in range(count)]
    for cp in cps:
        cp.start()
    for cp in cps:
        cp.wait()


def solution(mesh):
    leaves, dofs, blks = (mesh.shape[a] for a in ("leaf", "dof", "blk"))

    def body(modes, stiffness, density, eigen_blocks, parent):
        _, rows, layers, cy, cz = modes.shape
        n_modes = rows * blks
        cells = cy * cz
        others = blks - 1
        dma = pltpu.SemaphoreType.DMA
        any_spec = pl.BlockSpec(memory_space=pl.ANY)
        vmem_spec = pl.BlockSpec(memory_space=pltpu.VMEM)
        shapes = (
            jax.ShapeDtypeStruct((leaves // 2, rows, n_modes), F32),
            jax.ShapeDtypeStruct((rows, n_modes), F32),
            jax.ShapeDtypeStruct((rows, layers, cy, cz), BF16),
        )
        results = pl.pallas_call(
            lambda *refs: kernel((leaves, dofs, blks), FIRST_PART, *refs),
            out_shape=tuple(pltpu.VMEM(s.shape, s.dtype) for s in shapes),
            in_specs=[any_spec] * 5,
            out_specs=(any_spec,) * 3,
            scratch_shapes=[
                pltpu.SMEM((leaves,), jnp.int32),
                pltpu.VMEM((leaves // 2, rows, n_modes), F32),
                pltpu.VMEM((rows, n_modes), F32),
                pltpu.VMEM((rows, layers, cy, cz), BF16),
                pltpu.VMEM((layers, cy, cz), F32),
                pltpu.VMEM((2, cy, cz), F32),
                pltpu.VMEM((2, blks // 2, rows, n_modes), BF16),
                pltpu.VMEM((2, n_modes, cy, cz), BF16),
                pltpu.VMEM((n_modes * cy, cz), F32),
                pltpu.VMEM((2, n_modes, cells), BF16),
                pltpu.VMEM((n_modes, cells), BF16),
                pltpu.VMEM((n_modes * cy, cz), F32),
                pltpu.VMEM((2, n_modes, cy, cz), BF16),
                pltpu.VMEM((2, n_modes, cells // 2), BF16),
                pltpu.VMEM((n_modes, n_modes), F32),
                pltpu.VMEM((blks, rows, n_modes), BF16),
                pltpu.VMEM((others, rows, n_modes), BF16),
                pltpu.VMEM((1, n_modes), F32),
                pltpu.VMEM((others, 1, n_modes), F32),
                pltpu.VMEM((2 * rows, n_modes), F32),
                pltpu.VMEM((leaves * dofs, 2 * rows, n_modes), F32),
                dma((6,)),
                dma((2,)),
                dma(()),
                dma((2,)),
                dma((5,)),
                dma((9,)),
                pltpu.SemaphoreType.REGULAR((blks // 4,)),
                pltpu.SemaphoreType.REGULAR((leaves // 2 + dofs // 2,)),
            ],
            compiler_params=pltpu.CompilerParams(
                collective_id=0, has_side_effects=True
            ),
            name="tree",
        )(modes, stiffness, density, jnp.swapaxes(eigen_blocks, 1, 2), parent)
        node, root, vectors = pl.pallas_call(
            finish,
            out_shape=shapes,
            in_specs=[vmem_spec] * 3,
            out_specs=(any_spec,) * 3,
            scratch_shapes=[dma((3,))],
            compiler_params=pltpu.CompilerParams(vmem_limit_bytes=4 << 20),
            name="finish",
        )(*results)
        return node, root, vectors[None]

    in_specs = (
        P("leaf", "blk", "dof", None, None),
        P("leaf", "dof", None, None),
        P("leaf", "dof", None, None),
        P("leaf", None, "blk"),
        P(),
    )
    out_specs = (P(None, "blk", None), P("blk", None), P("leaf", "blk", "dof", None, None))
    return jax.shard_map(body, mesh=mesh, in_specs=in_specs, out_specs=out_specs, check_vma=False)
```

```python
import jax
import jax.numpy as jnp
from jax import lax
from jax.experimental import pallas as pl
from jax.experimental.pallas import tpu as pltpu
from jax.sharding import PartitionSpec as P

MESH = pl.DeviceIdType.MESH
F32 = jnp.float32
BF16 = jnp.bfloat16
FIRST_PART = 8
IN_PART = 12


def ring_peers(chips):
    found = {}
    for dz in range(chips):
        for dc in range(2):
            if dz or dc:
                found.setdefault(min(dz, chips - dz) + dc, []).append((dz, dc))
    return [found[d] for d in sorted(found)]


def drain(ref, sem):
    pltpu.make_async_copy(ref, ref, sem).wait()


def kernel(
    sizes,
    first_part,
    modes,
    stiffness,
    density,
    eigen,
    parent_in,
    node_out,
    root_out,
    vec_out,
    parent,
    node,
    root_sum,
    own,
    dens,
    coef,
    eig,
    land,
    wide,
    phi,
    lhs,
    tall,
    vecs,
    edge,
    kfull,
    ksend,
    kland,
    msend,
    mland,
    psend,
    pland,
    load_sem,
    in_recv,
    out_recv,
    h_recv,
    small_recv,
    send_sem,
    near_sem,
    plane_sem,
):
    leaves, dofs, blks = sizes
    chips = blks // 2
    rows, layers, cy, cz = own.shape
    n_modes = rows * blks
    half = cy // 2
    x, y, b = lax.axis_index("leaf"), lax.axis_index("dof"), lax.axis_index("blk")
    z, c = b // 2, lax.rem(b, 2)
    e_recv, k_recv, m_recv, p_recv, f_recv = (small_recv.at[i] for i in range(5))
    in_send, e_send, out_send, k_send, m_send, p_send, h0_send, h1_send, f_send = (send_sem.at[i] for i in range(9))
    my_rows = pl.ds(pl.multiple_of(b * rows, rows), rows)

    def layer_of(zz, cc, h):
        return 4 * zz + (3 * cc if h == 0 else 1 + cc)

    def column_peer(dz, dc):
        zz = lax.rem(z + dz, chips)
        cc = 1 - c if dc else c
        return zz, cc, zz * 2 + cc

    rings = [[column_peer(dz, dc) for dz, dc in ring] for ring in ring_peers(chips)]
    peers = [p for ring in rings for p in ring]
    plane = [(i, j) for i in range(leaves) for j in range(dofs) if (i, j) != (0, 0)]
    plane = [(lax.rem(x + i, leaves), lax.rem(y + j, dofs)) for i, j in plane]

    step = 2 * c - 1
    pz = lax.rem(z + step + chips, chips)
    wraps = jnp.where(c == 1, jnp.where(z == chips - 1, 1, 0), jnp.where(z == 0, 1, 0))
    py = lax.rem(y + step * wraps + dofs, dofs)
    pb = pz * 2 + (1 - c)
    at_end = jnp.where(c == 1, jnp.where(y == dofs - 1, 1, 0), jnp.where(y == 0, 1, 0)) * wraps

    near = [{"blk": p} for _, _, p in rings[0]]
    beside = [
        {"leaf": lax.rem(x + 1, leaves)},
        {"leaf": lax.rem(x + leaves - 1, leaves)},
        {"dof": lax.rem(y + 1, dofs)},
        {"dof": lax.rem(y + dofs - 1, dofs)},
    ]

    def tell(sem, devices):
        for device in devices:
            pl.semaphore_signal(sem, inc=1, device_id=device, device_id_type=MESH)

    def ahead(sem, up):
        for axis, i, n in (("leaf", x, leaves), ("dof", y, dofs)):
            step, first, last = (1, 0, n - 1) if up else (-1, n - 1, 0)

            @pl.when(i != last)
            def _():
                tell(sem, [{axis: i + step}])

            @pl.when(i == first)
            def _():
                tell(sem, [{axis: last}])

    def one(condition):
        return jnp.where(condition, 1, 0)

    heard_up = one(x > 0) + one(x == leaves - 1) + one(y > 0) + one(y == dofs - 1)
    heard_down = 2 * 2 - heard_up

    barrier = pltpu.get_barrier_semaphore()
    tell(barrier, near)
    ahead(barrier, True)
    loads = [
        pltpu.make_async_copy(modes.at[0], own, load_sem.at[0]),
        pltpu.make_async_copy(density.at[0], dens, load_sem.at[1]),
        pltpu.make_async_copy(parent_in, parent, load_sem.at[2]),
        pltpu.make_async_copy(stiffness.at[0, pl.ds(layer_of(z, c, 0), 1)], coef.at[pl.ds(0, 1)], load_sem.at[3]),
        pltpu.make_async_copy(stiffness.at[0, pl.ds(layer_of(z, c, 1), 1)], coef.at[pl.ds(1, 1)], load_sem.at[3]),
    ]
    for cp in loads:
        cp.start()

    def remote(src, dst, send, recv, device):
        pltpu.make_async_remote_copy(src, dst, send, recv, device_id=device, device_id_type=MESH).start()

    def send_modes(h, peer):
        zz, cc, p = peer
        remote(modes.at[0, :, layer_of(zz, cc, h)], land.at[h, my_rows], in_send, in_recv.at[h], {"blk": p})

    pl.semaphore_wait(barrier, heard_up + len(near))
    early, late = [], []
    for r, ring in enumerate(rings):
        if r:
            pl.semaphore_wait(near_sem.at[r - 1], len(near))
        if r < len(rings) - 1:
            tell(near_sem.at[r], near)
        if r == 0:
            ahead(plane_sem.at[0], False)
        for peer in ring:
            send_modes(0, peer)
            if r == 0:
                send_modes(1, peer)
                early.append(peer)
            else:
                late.insert(0, peer)
        for zz, cc, p in ring:
            if cc is c:
                remote(eigen.at[0], eig.at[c, z], e_send, e_recv, {"blk": p})
    for h in range(2):
        pltpu.make_async_copy(modes.at[0, :, layer_of(z, c, h)], land.at[h, my_rows], in_recv.at[h]).start()
    pltpu.make_async_copy(eigen.at[0], eig.at[c, z], e_recv).start()
    for peer in late[:IN_PART]:
        send_modes(1, peer)

    loads[0].wait()
    loads[1].wait()

    def mass_step(i, acc):
        f = own[:, i].astype(F32)
        w = (dens[i][None] * f).astype(BF16).astype(F32)
        return acc + w * f

    acc = lax.fori_loop(0, layers, mass_step, jnp.zeros((rows, cy, cz), F32))
    mass = jnp.sum(jnp.sum(acc, axis=1), axis=1, keepdims=True)
    lane = lax.broadcasted_iota(jnp.int32, (rows, n_modes), 1)
    sub = lax.broadcasted_iota(jnp.int32, (rows, n_modes), 0)
    mine = lane == sub + b * rows
    mass_row = jnp.sum(jnp.where(mine, mass, 0.0), axis=0, keepdims=True)
    msend[...] = mass_row
    for n, (_, _, p) in enumerate(peers):
        remote(msend, mland.at[n], m_send, m_recv, {"blk": p})
    loads[2].wait()
    drain(coef, load_sem.at[3])
    def plane_round(r):
        tell(plane_sem.at[r], beside)
        pl.semaphore_wait(plane_sem.at[r], len(beside))


    @pl.when(heard_down > 0)
    def _():
        pl.semaphore_wait(plane_sem.at[0], heard_down)

    plane_round(1)

    last_lane = lax.broadcasted_iota(jnp.int32, (n_modes, cz), 1) == cz - 1

    def relayout(h):
        wide[...] = land[h].reshape(n_modes * cy, cz).astype(F32)
        for j in range(cy):
            phi[h, :, j * cz : (j + 1) * cz] = wide[pl.ds(j, n_modes, stride=cy), :].astype(BF16)

    def send_edge(h, send, device):
        part = phi.at[h, :, pl.ds(pl.multiple_of(c * half * cz, half * cz), half * cz)]
        remote(part, edge.at[h], send, h_recv.at[h], device)

    def block_of(zz, cc):
        return pl.ds(pl.multiple_of((cc * chips + zz) * rows, rows), rows)

    def expand(h):
        e = eig[...].astype(F32).reshape(n_modes, n_modes).astype(BF16)
        for j in range(0, cy, 2):
            v = jnp.dot(e, phi[h, :, j * cz : (j + 2) * cz], preferred_element_type=F32)
            tall[pl.ds(j, n_modes, stride=cy), :] = v[:, :cz]
            tall[pl.ds(j + 1, n_modes, stride=cy), :] = v[:, cz:]
        vecs[h] = tall[...].astype(BF16).reshape(n_modes, cy, cz)
        pltpu.make_async_copy(vecs.at[h, block_of(z, c)], vec_out.at[:, layer_of(z, c, h)], out_recv).start()

    def send_block(h, zz, cc):
        remote(vecs.at[h, block_of(zz, cc)], vec_out.at[:, layer_of(z, c, h)], out_send, out_recv, {"blk": zz * 2 + cc})

    def send_vectors(h, some, first=()):
        for place, (zz, cc, p) in enumerate(some):
            for at, chip in first:
                if at == place:

                    @pl.when(z != chip)
                    def _():
                        for core in range(2):
                            send_block(h, chip, core)

            if first:
                others = zz == zz
                for _, chip in first:
                    others = others & (zz != chip)

                @pl.when(others | (zz == z))
                def _():
                    send_block(h, zz, cc)

            else:
                send_block(h, zz, cc)

    def images(h, other):
        nxt = wide[pl.ds(0, n_modes, stride=cy), :]
        for j in range(cy):
            f = nxt
            s = coef[h, j : j + 1, :] + 6.0
            side = jnp.where(last_lane, 0.0, pltpu.roll(f, cz - 1, 1))
            if j + 1 < cy:
                nxt = wide[pl.ds(j + 1, n_modes, stride=cy), :]
                side = side + nxt
            if other is not None:
                side = side + phi[other, :, j * cz : (j + 1) * cz].astype(F32)
            lhs[:, j * cz : (j + 1) * cz] = (s * f - 2.0 * side).astype(BF16)
        return lax.dot_general(lhs[...], phi[h], (((1,), (1,)), ((), ())), preferred_element_type=F32)

    def edge_product(h):
        part = phi[h, :, pl.ds(pl.multiple_of((1 - c) * half * cz, half * cz), half * cz)]
        return lax.dot_general(edge[h], part, (((1,), (1,)), ((), ())), preferred_element_type=F32)

    out_order = peers[::-1]
    drain(land.at[0], in_recv.at[0])
    relayout(0)

    @pl.when(at_end == 0)
    def _():
        send_edge(0, h0_send, {"dof": py, "blk": pb})

    for peer in late[IN_PART:]:
        send_modes(1, peer)
    drain(eig.at[0], e_recv)
    remote(eig.at[c], eig.at[c], f_send, f_recv, {"blk": z * 2 + (1 - c)})
    kfull[...] = images(0, None)
    drain(eig.at[0], f_recv)
    expand(0)
    send_vectors(0, out_order[:first_part])
    for r in range(2, leaves // 2 + dofs // 2):
        plane_round(r)

    drain(land.at[1], in_recv.at[1])
    relayout(1)
    send_edge(1, h1_send, {"blk": z * 2 + (1 - c)})
    kfull[...] += images(1, 0)
    expand(1)

    @pl.when(at_end == 0)
    def _():
        drain(edge.at[0], h_recv.at[0])
        kfull[...] -= 2.0 * edge_product(0)

    drain(edge.at[1], h_recv.at[1])
    total = kfull[...] - 2.0 * edge_product(1)
    kfull[...] = 0.5 * (total + total.T)
    for i in range(blks):
        ksend[i] = kfull[i * rows : (i + 1) * rows, :].astype(BF16)
    for n, (_, _, p) in reversed(list(enumerate(peers))):
        remote(ksend.at[p], kland.at[n], k_send, k_recv, {"blk": p})
    send_vectors(0, out_order[first_part:])
    send_vectors(1, out_order, ((0, 0), (4, 1)))

    drain(mland, m_recv)
    mass_total = mass_row
    for n in range(blks - 1):
        mass_total = mass_total + mland[n]
    drain(kland, k_recv)
    k_total = ksend[b].astype(F32)
    for n in range(blks - 1):
        k_total = k_total + kland[n].astype(F32)
    psend[:rows] = k_total
    psend[rows:] = jnp.broadcast_to(mass_total, (rows, n_modes))
    slot = x * dofs + y
    for i, j in plane:
        remote(psend, pland.at[slot], p_send, p_recv, {"leaf": i, "dof": j})
    pland[slot] = psend[...]
    drain(pland.at[pl.ds(0, leaves * dofs - 1)], p_recv)

    per_leaf = []
    for i in range(leaves):
        t = pland[i * dofs]
        for j in range(1, dofs):
            t = t + pland[i * dofs + j]
        per_leaf.append(t)
    root = jnp.zeros((rows, n_modes), F32)
    for i_node in range(node.shape[0]):
        t = jnp.zeros((2 * rows, n_modes), F32)
        for i in range(leaves):
            t = t + jnp.where(parent[i] == i_node, 1.0, 0.0).astype(F32) * per_leaf[i]
        node[i_node] = t[:rows]
        scale = 1.0 / jnp.sqrt(t[rows:])
        scale_own = jnp.sum(jnp.where(mine, scale, 0.0), axis=1, keepdims=True)
        root = root + scale_own * t[:rows] * scale
    root_sum[...] = root
    results = [
        pltpu.make_async_copy(node, node_out, load_sem.at[4]),
        pltpu.make_async_copy(root_sum, root_out, load_sem.at[5]),
    ]
    for cp in results:
        cp.start()

    drain(modes.at[0, :, pl.ds(0, 2 * blks - 2)], in_send)
    drain(eig.at[0, pl.ds(0, chips - 1)], e_send)
    drain(eig.at[0], f_send)
    drain(kland, k_send)
    drain(mland, m_send)
    drain(pland.at[pl.ds(0, leaves * dofs - 1)], p_send)

    @pl.when(at_end == 0)
    def _():
        drain(edge.at[0], h0_send)

    drain(edge.at[1], h1_send)
    for cp in results:
        cp.wait()
    drain(modes.at[0, :, pl.ds(0, 2 * blks - 2)], out_send)
    drain(vec_out, out_recv)


def finish(*refs):
    count = len(refs) // 2
    sem = refs[-1]
    cps = [pltpu.make_async_copy(refs[i], refs[count + i], sem.at[i]) for i in range(count)]
    for cp in cps:
        cp.start()
    for cp in cps:
        cp.wait()


def solution(mesh):
    leaves, dofs, blks = (mesh.shape[a] for a in ("leaf", "dof", "blk"))

    def body(modes, stiffness, density, eigen_blocks, parent):
        _, rows, layers, cy, cz = modes.shape
        n_modes = rows * blks
        cells = cy * cz
        others = blks - 1
        dma = pltpu.SemaphoreType.DMA
        any_spec = pl.BlockSpec(memory_space=pl.ANY)
        vmem_spec = pl.BlockSpec(memory_space=pltpu.VMEM)
        shapes = (
            jax.ShapeDtypeStruct((leaves // 2, rows, n_modes), F32),
            jax.ShapeDtypeStruct((rows, n_modes), F32),
            jax.ShapeDtypeStruct((rows, layers, cy, cz), BF16),
        )
        results = pl.pallas_call(
            lambda *refs: kernel((leaves, dofs, blks), FIRST_PART, *refs),
            out_shape=tuple(pltpu.VMEM(s.shape, s.dtype) for s in shapes),
            in_specs=[any_spec] * 5,
            out_specs=(any_spec,) * 3,
            scratch_shapes=[
                pltpu.SMEM((leaves,), jnp.int32),
                pltpu.VMEM((leaves // 2, rows, n_modes), F32),
                pltpu.VMEM((rows, n_modes), F32),
                pltpu.VMEM((rows, layers, cy, cz), BF16),
                pltpu.VMEM((layers, cy, cz), F32),
                pltpu.VMEM((2, cy, cz), F32),
                pltpu.VMEM((2, blks // 2, rows, n_modes), BF16),
                pltpu.VMEM((2, n_modes, cy, cz), BF16),
                pltpu.VMEM((n_modes * cy, cz), F32),
                pltpu.VMEM((2, n_modes, cells), BF16),
                pltpu.VMEM((n_modes, cells), BF16),
                pltpu.VMEM((n_modes * cy, cz), F32),
                pltpu.VMEM((2, n_modes, cy, cz), BF16),
                pltpu.VMEM((2, n_modes, cells // 2), BF16),
                pltpu.VMEM((n_modes, n_modes), F32),
                pltpu.VMEM((blks, rows, n_modes), BF16),
                pltpu.VMEM((others, rows, n_modes), BF16),
                pltpu.VMEM((1, n_modes), F32),
                pltpu.VMEM((others, 1, n_modes), F32),
                pltpu.VMEM((2 * rows, n_modes), F32),
                pltpu.VMEM((leaves * dofs, 2 * rows, n_modes), F32),
                dma((6,)),
                dma((2,)),
                dma(()),
                dma((2,)),
                dma((5,)),
                dma((9,)),
                pltpu.SemaphoreType.REGULAR((blks // 4,)),
                pltpu.SemaphoreType.REGULAR((leaves // 2 + dofs // 2,)),
            ],
            compiler_params=pltpu.CompilerParams(
                collective_id=0, has_side_effects=True
            ),
            name="tree",
        )(modes, stiffness, density, jnp.swapaxes(eigen_blocks, 1, 2), parent)
        node, root, vectors = pl.pallas_call(
            finish,
            out_shape=shapes,
            in_specs=[vmem_spec] * 3,
            out_specs=(any_spec,) * 3,
            scratch_shapes=[dma((3,))],
            compiler_params=pltpu.CompilerParams(vmem_limit_bytes=4 << 20),
            name="finish",
        )(*results)
        return node, root, vectors[None]

    in_specs = (
        P("leaf", "blk", "dof", None, None),
        P("leaf", "dof", None, None),
        P("leaf", "dof", None, None),
        P("leaf", None, "blk"),
        P(),
    )
    out_specs = (P(None, "blk", None), P("blk", None), P("leaf", "blk", "dof", None, None))
    return jax.shard_map(body, mesh=mesh, in_specs=in_specs, out_specs=out_specs, check_vma=False)
```

```python
import jax
import jax.numpy as jnp
from jax import lax
from jax.experimental import pallas as pl
from jax.experimental.pallas import tpu as pltpu
from jax.sharding import PartitionSpec as P

MESH = pl.DeviceIdType.MESH
F32 = jnp.float32
BF16 = jnp.bfloat16
FIRST_PART = 8
IN_PART = 12


def ring_peers(chips):
    found = {}
    for dz in range(chips):
        for dc in range(2):
            if dz or dc:
                found.setdefault(min(dz, chips - dz) + dc, []).append((dz, dc))
    return [found[d] for d in sorted(found)]


def drain(ref, sem):
    pltpu.make_async_copy(ref, ref, sem).wait()


def kernel(
    sizes,
    first_part,
    modes,
    stiffness,
    density,
    eigen,
    parent_in,
    node_out,
    root_out,
    vec_out,
    parent,
    node,
    root_sum,
    own,
    dens,
    coef,
    eig,
    land,
    wide,
    phi,
    lhs,
    tall,
    vecs,
    edge,
    kfull,
    pair_out,
    pair_in,
    ksend,
    kland,
    msend,
    mland,
    psend,
    pland,
    load_sem,
    in_recv,
    out_recv,
    h_recv,
    small_recv,
    send_sem,
    near_sem,
    plane_sem,
):
    leaves, dofs, blks = sizes
    chips = blks // 2
    rows, layers, cy, cz = own.shape
    n_modes = rows * blks
    half = cy // 2
    x, y, b = lax.axis_index("leaf"), lax.axis_index("dof"), lax.axis_index("blk")
    z, c = b // 2, lax.rem(b, 2)
    e_recv, k_recv, m_recv, p_recv, f_recv, pair_recv = (small_recv.at[i] for i in range(6))
    in_send, e_send, out_send, k_send, m_send, p_send, h0_send, h1_send, f_send, pair_send = (
        send_sem.at[i] for i in range(10)
    )
    my_rows = pl.ds(pl.multiple_of(b * rows, rows), rows)

    def layer_of(zz, cc, h):
        return 4 * zz + (3 * cc if h == 0 else 1 + cc)

    def column_peer(dz, dc):
        zz = lax.rem(z + dz, chips)
        cc = 1 - c if dc else c
        return zz, cc, zz * 2 + cc

    rings = [[column_peer(dz, dc) for dz, dc in ring] for ring in ring_peers(chips)]
    peers = [p for ring in rings for p in ring]
    plane = [(i, j) for i in range(leaves) for j in range(dofs) if (i, j) != (0, 0)]
    plane = [(lax.rem(x + i, leaves), lax.rem(y + j, dofs)) for i, j in plane]

    step = 2 * c - 1
    pz = lax.rem(z + step + chips, chips)
    wraps = jnp.where(c == 1, jnp.where(z == chips - 1, 1, 0), jnp.where(z == 0, 1, 0))
    py = lax.rem(y + step * wraps + dofs, dofs)
    pb = pz * 2 + (1 - c)
    at_end = jnp.where(c == 1, jnp.where(y == dofs - 1, 1, 0), jnp.where(y == 0, 1, 0)) * wraps

    near = [{"blk": p} for _, _, p in rings[0]]
    beside = [
        {"leaf": lax.rem(x + 1, leaves)},
        {"leaf": lax.rem(x + leaves - 1, leaves)},
        {"dof": lax.rem(y + 1, dofs)},
        {"dof": lax.rem(y + dofs - 1, dofs)},
    ]

    def tell(sem, devices):
        for device in devices:
            pl.semaphore_signal(sem, inc=1, device_id=device, device_id_type=MESH)

    def ahead(sem, up):
        for axis, i, n in (("leaf", x, leaves), ("dof", y, dofs)):
            step, first, last = (1, 0, n - 1) if up else (-1, n - 1, 0)

            @pl.when(i != last)
            def _():
                tell(sem, [{axis: i + step}])

            @pl.when(i == first)
            def _():
                tell(sem, [{axis: last}])

    def one(condition):
        return jnp.where(condition, 1, 0)

    heard_up = one(x > 0) + one(x == leaves - 1) + one(y > 0) + one(y == dofs - 1)
    heard_down = 2 * 2 - heard_up

    barrier = pltpu.get_barrier_semaphore()
    tell(barrier, near)
    ahead(barrier, True)
    loads = [
        pltpu.make_async_copy(modes.at[0], own, load_sem.at[0]),
        pltpu.make_async_copy(density.at[0], dens, load_sem.at[1]),
        pltpu.make_async_copy(parent_in, parent, load_sem.at[2]),
        pltpu.make_async_copy(stiffness.at[0, pl.ds(layer_of(z, c, 0), 1)], coef.at[pl.ds(0, 1)], load_sem.at[3]),
        pltpu.make_async_copy(stiffness.at[0, pl.ds(layer_of(z, c, 1), 1)], coef.at[pl.ds(1, 1)], load_sem.at[3]),
    ]
    for cp in loads:
        cp.start()

    def remote(src, dst, send, recv, device):
        pltpu.make_async_remote_copy(src, dst, send, recv, device_id=device, device_id_type=MESH).start()

    def send_modes(h, peer):
        zz, cc, p = peer
        remote(modes.at[0, :, layer_of(zz, cc, h)], land.at[h, my_rows], in_send, in_recv.at[h], {"blk": p})

    pl.semaphore_wait(barrier, heard_up + len(near))
    early, late = [], []
    for r, ring in enumerate(rings):
        if r:
            pl.semaphore_wait(near_sem.at[r - 1], len(near))
        if r < len(rings) - 1:
            tell(near_sem.at[r], near)
        if r == 0:
            ahead(plane_sem.at[0], False)
        for peer in ring:
            send_modes(0, peer)
            if r == 0:
                send_modes(1, peer)
                early.append(peer)
            else:
                late.insert(0, peer)
        for zz, cc, p in ring:
            if cc is c:
                remote(eigen.at[0], eig.at[c, z], e_send, e_recv, {"blk": p})
    for h in range(2):
        pltpu.make_async_copy(modes.at[0, :, layer_of(z, c, h)], land.at[h, my_rows], in_recv.at[h]).start()
    pltpu.make_async_copy(eigen.at[0], eig.at[c, z], e_recv).start()
    for peer in late[:IN_PART]:
        send_modes(1, peer)

    loads[0].wait()
    loads[1].wait()

    def mass_step(i, acc):
        f = own[:, i].astype(F32)
        w = (dens[i][None] * f).astype(BF16).astype(F32)
        return acc + w * f

    acc = lax.fori_loop(0, layers, mass_step, jnp.zeros((rows, cy, cz), F32))
    mass = jnp.sum(jnp.sum(acc, axis=1), axis=1, keepdims=True)
    lane = lax.broadcasted_iota(jnp.int32, (rows, n_modes), 1)
    sub = lax.broadcasted_iota(jnp.int32, (rows, n_modes), 0)
    mine = lane == sub + b * rows
    mass_row = jnp.sum(jnp.where(mine, mass, 0.0), axis=0, keepdims=True)
    loads[2].wait()
    drain(coef, load_sem.at[3])
    def plane_round(r):
        tell(plane_sem.at[r], beside)
        pl.semaphore_wait(plane_sem.at[r], len(beside))


    @pl.when(heard_down > 0)
    def _():
        pl.semaphore_wait(plane_sem.at[0], heard_down)

    plane_round(1)

    last_lane = lax.broadcasted_iota(jnp.int32, (n_modes, cz), 1) == cz - 1

    def relayout(h):
        wide[...] = land[h].reshape(n_modes * cy, cz).astype(F32)
        for j in range(cy):
            phi[h, :, j * cz : (j + 1) * cz] = wide[pl.ds(j, n_modes, stride=cy), :].astype(BF16)

    def send_edge(h, send, device):
        part = phi.at[h, :, pl.ds(pl.multiple_of(c * half * cz, half * cz), half * cz)]
        remote(part, edge.at[h], send, h_recv.at[h], device)

    def block_of(zz, cc):
        return pl.ds(pl.multiple_of((cc * chips + zz) * rows, rows), rows)

    def expand(h):
        e = eig[...].astype(F32).reshape(n_modes, n_modes).astype(BF16)
        for j in range(0, cy, 2):
            v = jnp.dot(e, phi[h, :, j * cz : (j + 2) * cz], preferred_element_type=F32)
            tall[pl.ds(j, n_modes, stride=cy), :] = v[:, :cz]
            tall[pl.ds(j + 1, n_modes, stride=cy), :] = v[:, cz:]
        vecs[h] = tall[...].astype(BF16).reshape(n_modes, cy, cz)
        pltpu.make_async_copy(vecs.at[h, block_of(z, c)], vec_out.at[:, layer_of(z, c, h)], out_recv).start()

    def send_block(h, zz, cc):
        remote(vecs.at[h, block_of(zz, cc)], vec_out.at[:, layer_of(z, c, h)], out_send, out_recv, {"blk": zz * 2 + cc})

    def send_vectors(h, some, first=()):
        for place, (zz, cc, p) in enumerate(some):
            for at, chip in first:
                if at == place:

                    @pl.when(z != chip)
                    def _():
                        for core in range(2):
                            send_block(h, chip, core)

            if first:
                others = zz == zz
                for _, chip in first:
                    others = others & (zz != chip)

                @pl.when(others | (zz == z))
                def _():
                    send_block(h, zz, cc)

            else:
                send_block(h, zz, cc)

    def images(h, other):
        nxt = wide[pl.ds(0, n_modes, stride=cy), :]
        for j in range(cy):
            f = nxt
            s = coef[h, j : j + 1, :] + 6.0
            side = jnp.where(last_lane, 0.0, pltpu.roll(f, cz - 1, 1))
            if j + 1 < cy:
                nxt = wide[pl.ds(j + 1, n_modes, stride=cy), :]
                side = side + nxt
            if other is not None:
                side = side + phi[other, :, j * cz : (j + 1) * cz].astype(F32)
            lhs[:, j * cz : (j + 1) * cz] = (s * f - 2.0 * side).astype(BF16)
        return lax.dot_general(lhs[...], phi[h], (((1,), (1,)), ((), ())), preferred_element_type=F32)

    def edge_product(h):
        part = phi[h, :, pl.ds(pl.multiple_of((1 - c) * half * cz, half * cz), half * cz)]
        return lax.dot_general(edge[h], part, (((1,), (1,)), ((), ())), preferred_element_type=F32)

    out_order = peers[::-1]

    def toward(k, dc, sign):
        zz = lax.rem(z + sign * step * k + chips, chips)
        cc = 1 - c if dc else c
        return zz, cc, zz * 2 + cc

    away = [toward(k, dc, -1) for k in range(chips // 2 - 1, 0, -1) for dc in (1, 0)]
    along = [toward(k, dc, 1) for k in range(chips // 2 - 1, 0, -1) for dc in (1, 0)]
    across = [toward(chips // 2, dc, 1) for dc in (1, 0)]
    sibling = [column_peer(0, 1)]
    out0_order = across + along + away + sibling
    drain(land.at[0], in_recv.at[0])
    relayout(0)

    @pl.when(at_end == 0)
    def _():
        send_edge(0, h0_send, {"dof": py, "blk": pb})

    for peer in late[IN_PART:]:
        send_modes(1, peer)
    drain(eig.at[0], e_recv)
    remote(eig.at[c], eig.at[c], f_send, f_recv, {"blk": z * 2 + (1 - c)})
    kfull[...] = images(0, None)
    drain(eig.at[0], f_recv)
    expand(0)
    send_vectors(0, out0_order[:first_part])
    for r in range(2, leaves // 2 + dofs // 2):
        plane_round(r)

    drain(land.at[1], in_recv.at[1])
    relayout(1)
    send_edge(1, h1_send, {"blk": z * 2 + (1 - c)})
    kfull[...] += images(1, 0)
    expand(1)

    @pl.when(at_end == 0)
    def _():
        drain(edge.at[0], h_recv.at[0])
        kfull[...] -= 2.0 * edge_product(0)

    drain(edge.at[1], h_recv.at[1])
    total = kfull[...] - 2.0 * edge_product(1)
    kfull[...] = 0.5 * (total + total.T)

    def block_rows(zz, cc):
        return pl.ds(pl.multiple_of((zz * 2 + cc) * rows, rows), rows)

    for zz in range(chips):
        pair_out[zz] = kfull[block_rows(zz, 1 - c), :]
    pair_out[chips] = jnp.broadcast_to(mass_row, (rows, n_modes))
    remote(pair_out, pair_in, pair_send, pair_recv, {"blk": z * 2 + (1 - c)})
    drain(pair_in, pair_recv)
    for zz in range(chips):
        ksend[zz] = (kfull[block_rows(zz, c), :] + pair_in[zz]).astype(BF16)
    mass_pair = mass_row + pair_in[chips][:1]
    msend[...] = mass_pair
    same_core = [(zz, p) for zz, cc, p in peers[::-1] if cc is c]
    for n, (zz, p) in enumerate(same_core):
        remote(ksend.at[zz], kland.at[n], k_send, k_recv, {"blk": p})
        remote(msend, mland.at[n], m_send, m_recv, {"blk": p})
    send_vectors(0, out0_order[first_part:])
    send_vectors(1, out_order, ((0, 0), (3, 1), (7, 2)))

    drain(mland, m_recv)
    mass_total = mass_pair
    for n in range(chips - 1):
        mass_total = mass_total + mland[n]
    drain(kland, k_recv)
    k_total = ksend[z].astype(F32)
    for n in range(chips - 1):
        k_total = k_total + kland[n].astype(F32)
    psend[:rows] = k_total
    psend[rows:] = jnp.broadcast_to(mass_total, (rows, n_modes))
    slot = x * dofs + y
    for i, j in plane:
        remote(psend, pland.at[slot], p_send, p_recv, {"leaf": i, "dof": j})
    pland[slot] = psend[...]
    drain(pland.at[pl.ds(0, leaves * dofs - 1)], p_recv)

    per_leaf = []
    for i in range(leaves):
        t = pland[i * dofs]
        for j in range(1, dofs):
            t = t + pland[i * dofs + j]
        per_leaf.append(t)
    root = jnp.zeros((rows, n_modes), F32)
    for i_node in range(node.shape[0]):
        t = jnp.zeros((2 * rows, n_modes), F32)
        for i in range(leaves):
            t = t + jnp.where(parent[i] == i_node, 1.0, 0.0).astype(F32) * per_leaf[i]
        node[i_node] = t[:rows]
        scale = 1.0 / jnp.sqrt(t[rows:])
        scale_own = jnp.sum(jnp.where(mine, scale, 0.0), axis=1, keepdims=True)
        root = root + scale_own * t[:rows] * scale
    root_sum[...] = root
    results = [
        pltpu.make_async_copy(node, node_out, load_sem.at[4]),
        pltpu.make_async_copy(root_sum, root_out, load_sem.at[5]),
    ]
    for cp in results:
        cp.start()

    drain(modes.at[0, :, pl.ds(0, 2 * blks - 2)], in_send)
    drain(eig.at[0, pl.ds(0, chips - 1)], e_send)
    drain(eig.at[0], f_send)
    drain(kland, k_send)
    drain(pair_in, pair_send)
    drain(mland, m_send)
    drain(pland.at[pl.ds(0, leaves * dofs - 1)], p_send)

    @pl.when(at_end == 0)
    def _():
        drain(edge.at[0], h0_send)

    drain(edge.at[1], h1_send)
    for cp in results:
        cp.wait()
    drain(modes.at[0, :, pl.ds(0, 2 * blks - 2)], out_send)
    drain(vec_out, out_recv)


def finish(*refs):
    count = len(refs) // 2
    sem = refs[-1]
    cps = [pltpu.make_async_copy(refs[i], refs[count + i], sem.at[i]) for i in range(count)]
    for cp in cps:
        cp.start()
    for cp in cps:
        cp.wait()


def solution(mesh):
    leaves, dofs, blks = (mesh.shape[a] for a in ("leaf", "dof", "blk"))

    def body(modes, stiffness, density, eigen_blocks, parent):
        _, rows, layers, cy, cz = modes.shape
        n_modes = rows * blks
        cells = cy * cz
        others = blks // 2 - 1
        dma = pltpu.SemaphoreType.DMA
        any_spec = pl.BlockSpec(memory_space=pl.ANY)
        vmem_spec = pl.BlockSpec(memory_space=pltpu.VMEM)
        shapes = (
            jax.ShapeDtypeStruct((leaves // 2, rows, n_modes), F32),
            jax.ShapeDtypeStruct((rows, n_modes), F32),
            jax.ShapeDtypeStruct((rows, layers, cy, cz), BF16),
        )
        results = pl.pallas_call(
            lambda *refs: kernel((leaves, dofs, blks), FIRST_PART, *refs),
            out_shape=tuple(pltpu.VMEM(s.shape, s.dtype) for s in shapes),
            in_specs=[any_spec] * 5,
            out_specs=(any_spec,) * 3,
            scratch_shapes=[
                pltpu.SMEM((leaves,), jnp.int32),
                pltpu.VMEM((leaves // 2, rows, n_modes), F32),
                pltpu.VMEM((rows, n_modes), F32),
                pltpu.VMEM((rows, layers, cy, cz), BF16),
                pltpu.VMEM((layers, cy, cz), F32),
                pltpu.VMEM((2, cy, cz), F32),
                pltpu.VMEM((2, blks // 2, rows, n_modes), BF16),
                pltpu.VMEM((2, n_modes, cy, cz), BF16),
                pltpu.VMEM((n_modes * cy, cz), F32),
                pltpu.VMEM((2, n_modes, cells), BF16),
                pltpu.VMEM((n_modes, cells), BF16),
                pltpu.VMEM((n_modes * cy, cz), F32),
                pltpu.VMEM((2, n_modes, cy, cz), BF16),
                pltpu.VMEM((2, n_modes, cells // 2), BF16),
                pltpu.VMEM((n_modes, n_modes), F32),
                pltpu.VMEM((blks // 2 + 1, rows, n_modes), F32),
                pltpu.VMEM((blks // 2 + 1, rows, n_modes), F32),
                pltpu.VMEM((blks // 2, rows, n_modes), BF16),
                pltpu.VMEM((others, rows, n_modes), BF16),
                pltpu.VMEM((1, n_modes), F32),
                pltpu.VMEM((others, 1, n_modes), F32),
                pltpu.VMEM((2 * rows, n_modes), F32),
                pltpu.VMEM((leaves * dofs, 2 * rows, n_modes), F32),
                dma((6,)),
                dma((2,)),
                dma(()),
                dma((2,)),
                dma((6,)),
                dma((10,)),
                pltpu.SemaphoreType.REGULAR((blks // 4,)),
                pltpu.SemaphoreType.REGULAR((leaves // 2 + dofs // 2,)),
            ],
            compiler_params=pltpu.CompilerParams(
                collective_id=0, has_side_effects=True
            ),
            name="tree",
        )(modes, stiffness, density, jnp.swapaxes(eigen_blocks, 1, 2), parent)
        node, root, vectors = pl.pallas_call(
            finish,
            out_shape=shapes,
            in_specs=[vmem_spec] * 3,
            out_specs=(any_spec,) * 3,
            scratch_shapes=[dma((3,))],
            compiler_params=pltpu.CompilerParams(vmem_limit_bytes=4 << 20),
            name="finish",
        )(*results)
        return node, root, vectors[None]

    in_specs = (
        P("leaf", "blk", "dof", None, None),
        P("leaf", "dof", None, None),
        P("leaf", "dof", None, None),
        P("leaf", None, "blk"),
        P(),
    )
    out_specs = (P(None, "blk", None), P("blk", None), P("leaf", "blk", "dof", None, None))
    return jax.shard_map(body, mesh=mesh, in_specs=in_specs, out_specs=out_specs, check_vma=False)
```

```python
import jax
import jax.numpy as jnp
from jax import lax
from jax.experimental import pallas as pl
from jax.experimental.pallas import tpu as pltpu
from jax.sharding import PartitionSpec as P

MESH = pl.DeviceIdType.MESH
F32 = jnp.float32
BF16 = jnp.bfloat16
FIRST_PART = 8
IN_PART = 12


def ring_peers(chips):
    found = {}
    for dz in range(chips):
        for dc in range(2):
            if dz or dc:
                found.setdefault(min(dz, chips - dz) + dc, []).append((dz, dc))
    return [found[d] for d in sorted(found)]


def drain(ref, sem):
    pltpu.make_async_copy(ref, ref, sem).wait()


def kernel(
    sizes,
    first_part,
    modes,
    stiffness,
    density,
    eigen,
    parent_in,
    node_out,
    root_out,
    vec_out,
    parent,
    node,
    root_sum,
    own,
    dens,
    coef,
    eig,
    land,
    wide,
    phi,
    lhs,
    tall,
    vecs,
    edge,
    kfull,
    pair_out,
    pair_in,
    ksend,
    kland,
    msend,
    mland,
    psend,
    pland,
    load_sem,
    in_recv,
    out_recv,
    h_recv,
    small_recv,
    send_sem,
    near_sem,
    plane_sem,
):
    leaves, dofs, blks = sizes
    chips = blks // 2
    rows, layers, cy, cz = own.shape
    n_modes = rows * blks
    half = cy // 2
    x, y, b = lax.axis_index("leaf"), lax.axis_index("dof"), lax.axis_index("blk")
    z, c = b // 2, lax.rem(b, 2)
    e_recv, k_recv, m_recv, p_recv, f_recv, pair_recv = (small_recv.at[i] for i in range(6))
    in_send, e_send, out_send, k_send, m_send, p_send, h0_send, h1_send, f_send, pair_send = (
        send_sem.at[i] for i in range(10)
    )
    my_rows = pl.ds(pl.multiple_of(b * rows, rows), rows)

    def layer_of(zz, cc, h):
        return 4 * zz + (3 * cc if h == 0 else 1 + cc)

    def column_peer(dz, dc):
        zz = lax.rem(z + dz, chips)
        cc = 1 - c if dc else c
        return zz, cc, zz * 2 + cc

    rings = [[column_peer(dz, dc) for dz, dc in ring] for ring in ring_peers(chips)]
    peers = [p for ring in rings for p in ring]
    plane = [(i, j) for i in range(leaves) for j in range(dofs) if (i, j) != (0, 0)]
    plane = [(lax.rem(x + i, leaves), lax.rem(y + j, dofs)) for i, j in plane]

    step = 2 * c - 1
    pz = lax.rem(z + step + chips, chips)
    wraps = jnp.where(c == 1, jnp.where(z == chips - 1, 1, 0), jnp.where(z == 0, 1, 0))
    py = lax.rem(y + step * wraps + dofs, dofs)
    pb = pz * 2 + (1 - c)
    at_end = jnp.where(c == 1, jnp.where(y == dofs - 1, 1, 0), jnp.where(y == 0, 1, 0)) * wraps

    near = [{"blk": p} for _, _, p in rings[0]]
    beside = [
        {"leaf": lax.rem(x + 1, leaves)},
        {"leaf": lax.rem(x + leaves - 1, leaves)},
        {"dof": lax.rem(y + 1, dofs)},
        {"dof": lax.rem(y + dofs - 1, dofs)},
    ]

    def tell(sem, devices):
        for device in devices:
            pl.semaphore_signal(sem, inc=1, device_id=device, device_id_type=MESH)

    def ahead(sem, up):
        for axis, i, n in (("leaf", x, leaves), ("dof", y, dofs)):
            step, first, last = (1, 0, n - 1) if up else (-1, n - 1, 0)

            @pl.when(i != last)
            def _():
                tell(sem, [{axis: i + step}])

            @pl.when(i == first)
            def _():
                tell(sem, [{axis: last}])

    def one(condition):
        return jnp.where(condition, 1, 0)

    heard_up = one(x > 0) + one(x == leaves - 1) + one(y > 0) + one(y == dofs - 1)
    heard_down = 2 * 2 - heard_up

    barrier = pltpu.get_barrier_semaphore()
    tell(barrier, near)
    ahead(barrier, True)
    loads = [
        pltpu.make_async_copy(modes.at[0], own, load_sem.at[0]),
        pltpu.make_async_copy(density.at[0], dens, load_sem.at[1]),
        pltpu.make_async_copy(parent_in, parent, load_sem.at[2]),
        pltpu.make_async_copy(stiffness.at[0, pl.ds(layer_of(z, c, 0), 1)], coef.at[pl.ds(0, 1)], load_sem.at[3]),
        pltpu.make_async_copy(stiffness.at[0, pl.ds(layer_of(z, c, 1), 1)], coef.at[pl.ds(1, 1)], load_sem.at[3]),
    ]
    for cp in loads:
        cp.start()

    def remote(src, dst, send, recv, device):
        pltpu.make_async_remote_copy(src, dst, send, recv, device_id=device, device_id_type=MESH).start()

    def send_modes(h, peer):
        zz, cc, p = peer
        remote(modes.at[0, :, layer_of(zz, cc, h)], land.at[h, my_rows], in_send, in_recv.at[h], {"blk": p})

    pl.semaphore_wait(barrier, heard_up + len(near))
    early, late = [], []
    for r, ring in enumerate(rings):
        if r:
            pl.semaphore_wait(near_sem.at[r - 1], len(near))
        if r < len(rings) - 1:
            tell(near_sem.at[r], near)
        if r == 0:
            ahead(plane_sem.at[0], False)
        for peer in ring:
            send_modes(0, peer)
            if r == 0:
                send_modes(1, peer)
                early.append(peer)
            else:
                late.insert(0, peer)
        for zz, cc, p in ring:
            if cc is c:
                remote(eigen.at[0], eig.at[c, z], e_send, e_recv, {"blk": p})
    for h in range(2):
        pltpu.make_async_copy(modes.at[0, :, layer_of(z, c, h)], land.at[h, my_rows], in_recv.at[h]).start()
    pltpu.make_async_copy(eigen.at[0], eig.at[c, z], e_recv).start()
    for peer in late[:IN_PART]:
        send_modes(1, peer)

    loads[0].wait()
    loads[1].wait()

    def mass_step(i, acc):
        f = own[:, i].astype(F32)
        w = (dens[i][None] * f).astype(BF16).astype(F32)
        return acc + w * f

    acc = lax.fori_loop(0, layers, mass_step, jnp.zeros((rows, cy, cz), F32))
    mass = jnp.sum(jnp.sum(acc, axis=1), axis=1, keepdims=True)
    lane = lax.broadcasted_iota(jnp.int32, (rows, n_modes), 1)
    sub = lax.broadcasted_iota(jnp.int32, (rows, n_modes), 0)
    mine = lane == sub + b * rows
    mass_row = jnp.sum(jnp.where(mine, mass, 0.0), axis=0, keepdims=True)
    loads[2].wait()
    drain(coef, load_sem.at[3])
    def plane_round(r):
        tell(plane_sem.at[r], beside)
        pl.semaphore_wait(plane_sem.at[r], len(beside))


    @pl.when(heard_down > 0)
    def _():
        pl.semaphore_wait(plane_sem.at[0], heard_down)

    plane_round(1)

    last_lane = lax.broadcasted_iota(jnp.int32, (n_modes, cz), 1) == cz - 1

    def relayout(h):
        wide[...] = land[h].reshape(n_modes * cy, cz).astype(F32)
        for j in range(cy):
            phi[h, :, j * cz : (j + 1) * cz] = wide[pl.ds(j, n_modes, stride=cy), :].astype(BF16)

    def send_edge(h, send, device):
        part = phi.at[h, :, pl.ds(pl.multiple_of(c * half * cz, half * cz), half * cz)]
        remote(part, edge.at[h], send, h_recv.at[h], device)

    def block_of(zz, cc):
        return pl.ds(pl.multiple_of((cc * chips + zz) * rows, rows), rows)

    def expand(h):
        e = eig[...].astype(F32).reshape(n_modes, n_modes).astype(BF16)
        for j in range(0, cy, 2):
            v = jnp.dot(e, phi[h, :, j * cz : (j + 2) * cz], preferred_element_type=F32)
            tall[pl.ds(j, n_modes, stride=cy), :] = v[:, :cz]
            tall[pl.ds(j + 1, n_modes, stride=cy), :] = v[:, cz:]
        vecs[h] = tall[...].astype(BF16).reshape(n_modes, cy, cz)
        pltpu.make_async_copy(vecs.at[h, block_of(z, c)], vec_out.at[:, layer_of(z, c, h)], out_recv).start()

    def send_block(h, zz, cc):
        remote(vecs.at[h, block_of(zz, cc)], vec_out.at[:, layer_of(z, c, h)], out_send, out_recv, {"blk": zz * 2 + cc})

    def send_vectors(h, some, first=()):
        for place, (zz, cc, p) in enumerate(some):
            for at, chip in first:
                if at == place:

                    @pl.when(z != chip)
                    def _():
                        for core in range(2):
                            send_block(h, chip, core)

            if first:
                others = zz == zz
                for _, chip in first:
                    others = others & (zz != chip)

                @pl.when(others | (zz == z))
                def _():
                    send_block(h, zz, cc)

            else:
                send_block(h, zz, cc)

    def images(h, other):
        nxt = wide[pl.ds(0, n_modes, stride=cy), :]
        for j in range(cy):
            f = nxt
            s = coef[h, j : j + 1, :] + 6.0
            side = jnp.where(last_lane, 0.0, pltpu.roll(f, cz - 1, 1))
            if j + 1 < cy:
                nxt = wide[pl.ds(j + 1, n_modes, stride=cy), :]
                side = side + nxt
            if other is not None:
                side = side + phi[other, :, j * cz : (j + 1) * cz].astype(F32)
            lhs[:, j * cz : (j + 1) * cz] = (s * f - 2.0 * side).astype(BF16)
        return lax.dot_general(lhs[...], phi[h], (((1,), (1,)), ((), ())), preferred_element_type=F32)

    def edge_product(h):
        part = phi[h, :, pl.ds(pl.multiple_of((1 - c) * half * cz, half * cz), half * cz)]
        return lax.dot_general(edge[h], part, (((1,), (1,)), ((), ())), preferred_element_type=F32)

    out_order = peers[::-1]

    def toward(k, dc, sign):
        zz = lax.rem(z + sign * step * k + chips, chips)
        cc = 1 - c if dc else c
        return zz, cc, zz * 2 + cc

    away = [toward(k, dc, -1) for k in range(chips // 2 - 1, 0, -1) for dc in (1, 0)]
    along = [toward(k, dc, 1) for k in range(chips // 2 - 1, 0, -1) for dc in (1, 0)]
    across = [toward(chips // 2, dc, 1) for dc in (1, 0)]
    sibling = [column_peer(0, 1)]
    out0_order = across + along + away + sibling
    drain(land.at[0], in_recv.at[0])
    relayout(0)

    @pl.when(at_end == 0)
    def _():
        send_edge(0, h0_send, {"dof": py, "blk": pb})

    for peer in late[IN_PART:]:
        send_modes(1, peer)
    drain(eig.at[0], e_recv)
    remote(eig.at[c], eig.at[c], f_send, f_recv, {"blk": z * 2 + (1 - c)})
    kfull[...] = images(0, None)
    drain(eig.at[0], f_recv)
    expand(0)
    send_vectors(0, out0_order[:first_part])
    for r in range(2, leaves // 2 + dofs // 2):
        plane_round(r)

    drain(land.at[1], in_recv.at[1])
    relayout(1)
    send_edge(1, h1_send, {"blk": z * 2 + (1 - c)})
    kfull[...] += images(1, 0)
    expand(1)

    @pl.when(at_end == 0)
    def _():
        drain(edge.at[0], h_recv.at[0])
        kfull[...] -= 2.0 * edge_product(0)

    drain(edge.at[1], h_recv.at[1])
    total = kfull[...] - 2.0 * edge_product(1)
    kfull[...] = 0.5 * (total + total.T)

    def block_rows(zz, cc):
        return pl.ds(pl.multiple_of((zz * 2 + cc) * rows, rows), rows)

    for zz in range(chips):
        pair_out[zz] = kfull[block_rows(zz, 1 - c), :]
    pair_out[chips] = jnp.broadcast_to(mass_row, (rows, n_modes))
    remote(pair_out, pair_in, pair_send, pair_recv, {"blk": z * 2 + (1 - c)})
    drain(pair_in, pair_recv)
    for zz in range(chips):
        ksend[zz] = (kfull[block_rows(zz, c), :] + pair_in[zz]).astype(BF16)
    mass_pair = mass_row + pair_in[chips][:1]
    msend[...] = mass_pair
    same_core = [(zz, p) for zz, cc, p in peers[::-1] if cc is c]
    for n, (zz, p) in enumerate(same_core):
        remote(ksend.at[zz], kland.at[n], k_send, k_recv, {"blk": p})
        remote(msend, mland.at[n], m_send, m_recv, {"blk": p})
    send_vectors(0, out0_order[first_part:])
    send_vectors(1, out_order, ((0, 0), (2, 1), (5, 2), (9, 3)))

    drain(mland, m_recv)
    mass_total = mass_pair
    for n in range(chips - 1):
        mass_total = mass_total + mland[n]
    drain(kland, k_recv)
    k_total = ksend[z].astype(F32)
    for n in range(chips - 1):
        k_total = k_total + kland[n].astype(F32)
    psend[:rows] = k_total
    psend[rows:] = jnp.broadcast_to(mass_total, (rows, n_modes))
    slot = x * dofs + y
    for i, j in plane:
        remote(psend, pland.at[slot], p_send, p_recv, {"leaf": i, "dof": j})
    pland[slot] = psend[...]
    drain(pland.at[pl.ds(0, leaves * dofs - 1)], p_recv)

    per_leaf = []
    for i in range(leaves):
        t = pland[i * dofs]
        for j in range(1, dofs):
            t = t + pland[i * dofs + j]
        per_leaf.append(t)
    root = jnp.zeros((rows, n_modes), F32)
    for i_node in range(node.shape[0]):
        t = jnp.zeros((2 * rows, n_modes), F32)
        for i in range(leaves):
            t = t + jnp.where(parent[i] == i_node, 1.0, 0.0).astype(F32) * per_leaf[i]
        node[i_node] = t[:rows]
        scale = 1.0 / jnp.sqrt(t[rows:])
        scale_own = jnp.sum(jnp.where(mine, scale, 0.0), axis=1, keepdims=True)
        root = root + scale_own * t[:rows] * scale
    root_sum[...] = root
    results = [
        pltpu.make_async_copy(node, node_out, load_sem.at[4]),
        pltpu.make_async_copy(root_sum, root_out, load_sem.at[5]),
    ]
    for cp in results:
        cp.start()

    drain(modes.at[0, :, pl.ds(0, 2 * blks - 2)], in_send)
    drain(eig.at[0, pl.ds(0, chips - 1)], e_send)
    drain(eig.at[0], f_send)
    drain(kland, k_send)
    drain(pair_in, pair_send)
    drain(mland, m_send)
    drain(pland.at[pl.ds(0, leaves * dofs - 1)], p_send)

    @pl.when(at_end == 0)
    def _():
        drain(edge.at[0], h0_send)

    drain(edge.at[1], h1_send)
    for cp in results:
        cp.wait()
    drain(modes.at[0, :, pl.ds(0, 2 * blks - 2)], out_send)
    drain(vec_out, out_recv)


def finish(*refs):
    count = len(refs) // 2
    sem = refs[-1]
    cps = [pltpu.make_async_copy(refs[i], refs[count + i], sem.at[i]) for i in range(count)]
    for cp in cps:
        cp.start()
    for cp in cps:
        cp.wait()


def solution(mesh):
    leaves, dofs, blks = (mesh.shape[a] for a in ("leaf", "dof", "blk"))

    def body(modes, stiffness, density, eigen_blocks, parent):
        _, rows, layers, cy, cz = modes.shape
        n_modes = rows * blks
        cells = cy * cz
        others = blks // 2 - 1
        dma = pltpu.SemaphoreType.DMA
        any_spec = pl.BlockSpec(memory_space=pl.ANY)
        vmem_spec = pl.BlockSpec(memory_space=pltpu.VMEM)
        shapes = (
            jax.ShapeDtypeStruct((leaves // 2, rows, n_modes), F32),
            jax.ShapeDtypeStruct((rows, n_modes), F32),
            jax.ShapeDtypeStruct((rows, layers, cy, cz), BF16),
        )
        results = pl.pallas_call(
            lambda *refs: kernel((leaves, dofs, blks), FIRST_PART, *refs),
            out_shape=tuple(pltpu.VMEM(s.shape, s.dtype) for s in shapes),
            in_specs=[any_spec] * 5,
            out_specs=(any_spec,) * 3,
            scratch_shapes=[
                pltpu.SMEM((leaves,), jnp.int32),
                pltpu.VMEM((leaves // 2, rows, n_modes), F32),
                pltpu.VMEM((rows, n_modes), F32),
                pltpu.VMEM((rows, layers, cy, cz), BF16),
                pltpu.VMEM((layers, cy, cz), F32),
                pltpu.VMEM((2, cy, cz), F32),
                pltpu.VMEM((2, blks // 2, rows, n_modes), BF16),
                pltpu.VMEM((2, n_modes, cy, cz), BF16),
                pltpu.VMEM((n_modes * cy, cz), F32),
                pltpu.VMEM((2, n_modes, cells), BF16),
                pltpu.VMEM((n_modes, cells), BF16),
                pltpu.VMEM((n_modes * cy, cz), F32),
                pltpu.VMEM((2, n_modes, cy, cz), BF16),
                pltpu.VMEM((2, n_modes, cells // 2), BF16),
                pltpu.VMEM((n_modes, n_modes), F32),
                pltpu.VMEM((blks // 2 + 1, rows, n_modes), F32),
                pltpu.VMEM((blks // 2 + 1, rows, n_modes), F32),
                pltpu.VMEM((blks // 2, rows, n_modes), BF16),
                pltpu.VMEM((others, rows, n_modes), BF16),
                pltpu.VMEM((1, n_modes), F32),
                pltpu.VMEM((others, 1, n_modes), F32),
                pltpu.VMEM((2 * rows, n_modes), F32),
                pltpu.VMEM((leaves * dofs, 2 * rows, n_modes), F32),
                dma((6,)),
                dma((2,)),
                dma(()),
                dma((2,)),
                dma((6,)),
                dma((10,)),
                pltpu.SemaphoreType.REGULAR((blks // 4,)),
                pltpu.SemaphoreType.REGULAR((leaves // 2 + dofs // 2,)),
            ],
            compiler_params=pltpu.CompilerParams(
                collective_id=0, has_side_effects=True
            ),
            name="tree",
        )(modes, stiffness, density, jnp.swapaxes(eigen_blocks, 1, 2), parent)
        node, root, vectors = pl.pallas_call(
            finish,
            out_shape=shapes,
            in_specs=[vmem_spec] * 3,
            out_specs=(any_spec,) * 3,
            scratch_shapes=[dma((3,))],
            compiler_params=pltpu.CompilerParams(vmem_limit_bytes=4 << 20),
            name="finish",
        )(*results)
        return node, root, vectors[None]

    in_specs = (
        P("leaf", "blk", "dof", None, None),
        P("leaf", "dof", None, None),
        P("leaf", "dof", None, None),
        P("leaf", None, "blk"),
        P(),
    )
    out_specs = (P(None, "blk", None), P("blk", None), P("leaf", "blk", "dof", None, None))
    return jax.shard_map(body, mesh=mesh, in_specs=in_specs, out_specs=out_specs, check_vma=False)
```
